32 devices in a mesh: groups: 2 (over y), hidden: 4 (over z), cols: 2 (over x), rep: 2 (over core).
Axes of the slice: x: 2, y: 2, z: 4, core: 2. Of those that a mesh axis runs over, the one named last changes fastest.
Arguments:
- inputs: bfloat16 [8192, 28672], P(('groups', 'cols', 'rep'), 'hidden'), parts along dimension 0, may hold values from -6 to 6
- grads: bfloat16 [8192, 8192], P(('groups', 'cols', 'rep'), 'hidden'), parts along dimension 0, may hold values from -1.5 to 1.5
- in_signs: int32 [28672], P('hidden'), may hold values from -1 to 1, as said below
- out_signs: int32 [8192], P('hidden'), may hold values from -1 to 1, as said below
- in_rows: int32 [128], replicated, may hold values from 0 to 28671, as said below
- out_rows: int32 [128], replicated, may hold values from 0 to 8191, as said below
- inv_gram: bfloat16 [16384, 16384], P('hidden', ('cols', 'rep')), may hold values from -0.0625 to 0.0625
Outputs:
- preconditioned: float32 [64, 16384], P('groups', ('cols', 'rep', 'hidden')), parts along dimension 0
The draws below stay inside these ranges and needn't reach their ends.
There are 2 independent parts, one for each index of `groups`. The reference program is written for one: setup_inputs(seed, part) draws one part's arguments, and reference() takes and returns one part's arrays. A program takes and returns all parts, laid end to end along the dimension named above; an argument that names none is the same for every part. Nothing has to cross between parts.
Inputs may be any that keep to these rules, and one draw needn't show every extreme that they name: `in_signs`: each entry is -1 or +1. `out_signs`: each entry is -1 or +1. `in_rows`: distinct. `out_rows`: distinct.
All inputs are finite; a program needn't handle non-finite values.
Results may differ from the reference program's by a relative error of at most 0.0003.
Values sent between devices are 32-bit elements; how exact they have to be, the bound alone decides.
A program may use at most 128 MiB of HBM per device.

```python
import math
import jax
import jax.numpy as jnp
from jax import lax

IN_W = 28672
OUT_W = 8192
HAD = 64
SKETCH = 128
SEQ = 128
GRAM = 16384
TOKENS = 4096


def draw_in_signs(key, part):
    return (2 * jax.random.randint(jax.random.fold_in(key, 101), (IN_W,), 0, 2) - 1).astype(jnp.int32)


def draw_out_signs(key, part):
    return (2 * jax.random.randint(jax.random.fold_in(key, 202), (OUT_W,), 0, 2) - 1).astype(jnp.int32)


def draw_in_rows(key, part):
    return jax.random.permutation(jax.random.fold_in(key, 303), IN_W)[:SKETCH].astype(jnp.int32)


def draw_out_rows(key, part):
    return jax.random.permutation(jax.random.fold_in(key, 404), OUT_W)[:SKETCH].astype(jnp.int32)


def spiked(drawn, own_key, source, target, shards_of, factor):
    def block_of(axis_at):
        return (jnp.arange(drawn.shape[axis_at]) // (drawn.shape[axis_at] // shards_of)).reshape((-1,) + (1,) * (drawn.ndim - 1 - axis_at))

    first = jax.random.permutation(own_key, shards_of)[block_of(target)]
    second = (block_of(target) + shards_of // 2) % shards_of
    return jnp.where((block_of(source) == first) | (block_of(source) == second), factor * drawn, drawn)


def level_of(own_key, dims, split, least, top_value):
    def one(position, blocks):
        steps = jax.random.uniform(jax.random.fold_in(jax.random.fold_in(own_key, 6), position), (blocks,), jnp.float32, least / len(split), top_value / len(split))
        return jnp.repeat(jnp.exp(steps), dims[position] // blocks).reshape((-1,) + (1,) * (len(dims) - position - 1))

    level = one(*split[0])
    for cut in split[1:]:
        level = level * one(*cut)
    return level


def scatter_about(key, dims, scale, reach, shards=(), held_as=jnp.bfloat16):
    values = jax.random.normal(key, dims, jnp.float32) * scale
    if len(shards) > 0:
        values = level_of(key, dims, shards, -0.22, 0.18) * values
    return jnp.clip(values, min=-reach, max=reach).astype(held_as)


def gaussian_with(key, extent, deviation, most, cuts, heavy, kind=jnp.bfloat16):
    array = deviation * jax.random.normal(key, extent, jnp.float32)
    if cuts:
        array = array * level_of(key, extent, cuts, -0.22, 0.18)
    return jnp.clip(spiked(array, jax.random.fold_in(key, 3), *heavy), -most, most).astype(kind)


def setup_inputs(seed: int = 0, part: int = 0) -> dict:
    key_list = jax.random.split(jax.random.key(seed), 8)
    own_keys = jax.random.split(jax.random.fold_in(key_list[7], part), 8)
    return {
        "inputs": scatter_about(own_keys[0], (TOKENS, IN_W), 1.0, 6.0, ((0, 4), (1, 4))),
        "grads": scatter_about(own_keys[1], (TOKENS, OUT_W), 0.25, 1.5, ((0, 4), (1, 4))),
        "in_signs": draw_in_signs(jax.random.fold_in(key_list[7], 71), part),
        "out_signs": draw_out_signs(jax.random.fold_in(key_list[7], 71), part),
        "in_rows": draw_in_rows(jax.random.fold_in(key_list[7], 71), part),
        "out_rows": draw_out_rows(jax.random.fold_in(key_list[7], 71), part),
        "inv_gram": gaussian_with(key_list[6], (GRAM, GRAM), GRAM ** -0.5, 0.0625, ((0, 4), (1, 4)), (0, 1, 4, 2.0)),
    }


def had_sign(left, right):
    both = jnp.bitwise_and(left, right)
    count = jnp.zeros(both.shape, jnp.int32)
    for bit in range(HAD.bit_length() - 1):
        count = count + jnp.bitwise_and(jnp.right_shift(both, bit), 1)
    return (1 - 2 * (count % 2)).astype(jnp.float32)

def sketch(values, signs, rows, width):
    inner = width // HAD
    row_high = (rows // inner).astype(jnp.int32)
    row_low = (rows % inner).astype(jnp.int32)
    cube = values.reshape(values.shape[0], HAD, inner)
    sign_grid = signs.reshape(HAD, inner)
    picked = jnp.take(cube, row_low, axis=2).astype(jnp.float32)
    sources = jnp.arange(HAD, dtype=jnp.int32)
    coef = had_sign(row_high[None, :], sources[:, None]) * jnp.take(sign_grid, row_low, axis=1).astype(jnp.float32) / math.sqrt(HAD)
    return jnp.einsum('thk,hk->tk', picked, coef)

def reference(inputs, grads, in_signs, out_signs, in_rows, out_rows, inv_gram):
    out_sketch = sketch(grads, out_signs, out_rows, OUT_W)
    in_sketch = sketch(inputs, in_signs, in_rows, IN_W)
    count = out_sketch.shape[0] // SEQ
    projected = jnp.einsum('esp,esq->epq', out_sketch.reshape(count, SEQ, SKETCH), in_sketch.reshape(count, SEQ, SKETCH), precision=lax.Precision.HIGHEST)
    projected = projected.reshape(count, GRAM)
    return jnp.dot(projected, inv_gram.astype(jnp.float32), precision=lax.Precision.HIGHEST, preferred_element_type=jnp.float32)
```

```python
import functools
import math

import jax
import jax.numpy as jnp
from jax import lax
from jax.experimental import pallas as pl
from jax.experimental.pallas import tpu as pltpu
from jax.sharding import PartitionSpec as P

IN_W = 28672
OUT_W = 8192
HAD = 64
SKETCH = 128
SEQ = 128
LANES = 128
HIDDEN = 4
STEP = 512
MESH = pl.DeviceIdType.MESH


def had_parity(left, right):
    both = jnp.bitwise_and(left, right)
    for shift in (4, 2, 1):
        both = jnp.bitwise_xor(both, jnp.right_shift(both, shift))
    return jnp.bitwise_and(both, 1)


def split_rows(rows, inner):
    high = jnp.floor((rows.astype(jnp.float32) + 0.5) * (1.0 / inner)).astype(jnp.int32)
    return high, rows - high * inner


def build_matrix(rows_ref, sign_ref, out_ref, shard, width):
    inner = width // HAD
    local_high = out_ref.shape[0] // inner
    high, low = split_rows(rows_ref[...], inner)
    hit = lax.broadcasted_iota(jnp.int32, (inner, SKETCH), 0) == low
    onehot = jnp.where(hit, 1.0, 0.0)
    sign = sign_ref[...].astype(jnp.float32).astype(jnp.bfloat16)
    line = lax.broadcasted_iota(jnp.int32, (sign.shape[0], SKETCH), 0)
    lane = lax.broadcasted_iota(jnp.int32, (LANES, SKETCH), 0)
    picked = {}
    for h in range(local_high):
        first, offset = divmod(h * inner, LANES)
        at = offset + low
        if offset not in picked:
            pick = jnp.where(lane == jnp.bitwise_and(at, LANES - 1), 1.0, 0.0).astype(jnp.bfloat16)
            picked[offset] = jnp.dot(sign, pick, preferred_element_type=jnp.float32)
        own = line == first + jnp.right_shift(at, LANES.bit_length() - 1)
        coef = jnp.sum(jnp.where(own, picked[offset], 0.0), axis=0, keepdims=True)
        parity = had_parity(high, shard * local_high + h)
        coef = coef * (1 - 2 * parity).astype(jnp.float32) * (1.0 / math.sqrt(HAD))
        out_ref[h * inner : (h + 1) * inner, :] = (onehot * coef).astype(jnp.bfloat16)


def fused_kernel(
    x_ref,
    g_ref,
    in_sign_ref,
    out_sign_ref,
    in_rows_ref,
    out_rows_ref,
    gram_ref,
    out_ref,
    x_buf,
    g_buf,
    gram_buf,
    mat_in,
    mat_out,
    part,
    land_edge,
    land_far,
    proj,
    allp,
    wide,
    psum,
    sum_edge,
    sum_far,
    x_sem,
    g_sem,
    gram_sem,
    send_part,
    recv_edge,
    recv_far,
    send_rows,
    send_fwd,
    recv_rows,
    send_core,
    recv_core,
    send_sum,
    recv_sum_edge,
    recv_sum_far,
):
    me = lax.axis_index("hidden")
    my_col = lax.axis_index("cols")
    my_rep = lax.axis_index("rep")
    count = x_buf.shape[0]
    side = me // 2
    mid = lax.rem((me + 1) // 2, 2)
    own_edge, own_mid, far_mid = 3 * side, 1 + side, 2 - side
    block_p = SKETCH // HIDDEN
    chunks = psum.shape[0]
    step_cols = psum.shape[2]

    def example(k):
        early = 1 - (k + count - 3) // count
        label = count - 1 - k + early * (2 * k - 2)
        return label + side * (count - 1 - 2 * label)

    def load_x(k):
        row = pl.multiple_of(example(k) * SEQ, SEQ)
        return pltpu.make_async_copy(x_ref.at[pl.ds(row, SEQ)], x_buf.at[k], x_sem.at[k])

    def load_g(k):
        row = pl.multiple_of(example(k) * SEQ, SEQ)
        return pltpu.make_async_copy(g_ref.at[pl.ds(row, SEQ)], g_buf.at[k], g_sem.at[k])

    gram_parts = gram_sem.shape[0]
    gram_rows = gram_ref.shape[0] // gram_parts

    def load_gram(k):
        where = pl.ds(k * gram_rows, gram_rows)
        return pltpu.make_async_copy(gram_ref.at[where], gram_buf.at[where], gram_sem.at[k])

    for k in range(count):
        load_g(k).start()
        load_x(k).start()

    barrier = pltpu.get_barrier_semaphore()
    pl.semaphore_signal(barrier, inc=1, device_id={"rep": 1 - my_rep}, device_id_type=MESH)
    for d in range(1, HIDDEN):
        pl.semaphore_signal(barrier, inc=1, device_id={"hidden": lax.rem(me + d, HIDDEN)}, device_id_type=MESH)
    for d in range(HIDDEN):
        pl.semaphore_signal(
            barrier, inc=1, device_id={"hidden": lax.rem(me + d, HIDDEN), "cols": 1 - my_col}, device_id_type=MESH
        )
    build_matrix(out_rows_ref, out_sign_ref, mat_out, me, OUT_W)
    build_matrix(in_rows_ref, in_sign_ref, mat_in, me, IN_W)
    pl.semaphore_wait(barrier, 2 * HIDDEN)

    def edge_send(k, h):
        return pltpu.make_async_remote_copy(
            src_ref=part.at[k, h],
            dst_ref=land_edge.at[k, h],
            send_sem=send_part.at[k, h],
            recv_sem=recv_edge.at[k, h],
            device_id={"hidden": own_mid},
            device_id_type=MESH,
        )

    def far_send(k, h):
        return pltpu.make_async_remote_copy(
            src_ref=part.at[k, h],
            dst_ref=land_far.at[k, h],
            send_sem=send_part.at[k, h],
            recv_sem=recv_far.at[k, h],
            device_id={"hidden": far_mid},
            device_id_type=MESH,
        )

    def home_send(j, h):
        return pltpu.make_async_remote_copy(
            src_ref=part.at[5 + j, h],
            dst_ref=land_far.at[j, h],
            send_sem=send_part.at[5 + j, h],
            recv_sem=recv_far.at[j, h],
            device_id={"hidden": own_edge},
            device_id_type=MESH,
        )

    def edge_arrived(k, h):
        return pltpu.make_async_remote_copy(
            src_ref=part.at[k, h],
            dst_ref=land_edge.at[k, h],
            send_sem=send_part.at[k, h],
            recv_sem=recv_edge.at[k, h],
            device_id={"rep": 1 - my_rep},
            device_id_type=MESH,
        )

    def far_arrived(k, h):
        return pltpu.make_async_remote_copy(
            src_ref=part.at[k, h],
            dst_ref=land_far.at[k, h],
            send_sem=send_part.at[k, h],
            recv_sem=recv_far.at[k, h],
            device_id={"rep": 1 - my_rep},
            device_id_type=MESH,
        )

    def relay_edge(n):
        k, h = n // 2, lax.rem(n, 2)
        edge_arrived(k, h).wait_recv()
        part[k, h] = part[k, h] + land_edge[k, h]
        far_send(k, h).start()

    def relay_home(n):
        j, h = n // 2, lax.rem(n, 2)
        far_arrived(j, h).wait_recv()
        part[5 + j, h] = part[5 + j, h] + land_far[j, h]
        home_send(j, h).start()

    def sketch_step(k, carry):
        sends = jnp.logical_and(mid == 0, k < 5)
        load_g(k).wait()
        part[k, 0] = jnp.dot(g_buf[k], mat_out[...], preferred_element_type=jnp.float32)

        @pl.when(sends)
        def _():
            edge_send(k, 0).start()

        load_x(k).wait()
        part[k, 1] = jnp.dot(x_buf[k], mat_in[...], preferred_element_type=jnp.float32)

        @pl.when(sends)
        def _():
            edge_send(k, 1).start()

        @pl.when(jnp.logical_and(mid == 1, k >= 5))
        def _():
            relay_edge(k - 5)

        return carry

    lax.fori_loop(0, count, sketch_step, 0)
    for k in range(gram_parts):
        load_gram(k).start()

    def project(k, slot):
        proj[slot] = lax.dot_general(
            part[k, 0],
            part[k, 1],
            (((0,), (0,)), ((), ())),
            precision=lax.Precision.HIGHEST,
            preferred_element_type=jnp.float32,
        )

    def place(rep, col, i):
        return (rep * 2 + col) * count + i

    def rows_copy(slot, i, d, c):
        z = lax.rem(me + d, HIDDEN)
        col = my_col + c * (1 - 2 * my_col)
        return pltpu.make_async_remote_copy(
            src_ref=proj.at[slot, pl.ds(pl.multiple_of(z * block_p, block_p), block_p), :],
            dst_ref=allp.at[place(my_rep, my_col, i)],
            send_sem=send_rows.at[slot, d, c],
            recv_sem=recv_rows.at[my_col, i],
            device_id={"hidden": z, "cols": col},
            device_id_type=MESH,
        )

    def forward(i, n):
        block = allp.at[place(my_rep, my_col, i)]
        return pltpu.make_async_remote_copy(
            src_ref=block,
            dst_ref=block,
            send_sem=send_fwd.at[n],
            recv_sem=recv_rows.at[my_col, i],
            device_id={"cols": 1 - my_col},
            device_id_type=MESH,
        )

    def rows_arrived(col, i):
        block = allp.at[place(my_rep, col, i)]
        return pltpu.make_async_remote_copy(
            src_ref=block,
            dst_ref=block,
            send_sem=send_fwd.at[0],
            recv_sem=recv_rows.at[col, i],
            device_id={"cols": 1 - my_col},
            device_id_type=MESH,
        )

    def row_sends(late):
        both = [(d, c) for d in range(HIDDEN) for c in range(2) if (d, c) != (0, 0)]
        return both if late else [(d, c) for d, c in both if d == 0 or c == 0]

    def distribute(slot, i, late):
        for d, c in row_sends(late):
            rows_copy(slot, i, d, c).start()
        allp[place(my_rep, my_col, i)] = proj[slot, pl.ds(pl.multiple_of(me * block_p, block_p), block_p), :]

    @pl.when(mid == 1)
    def _():
        def turn(n, carry):
            relay_home(n)
            relay_edge(n + 3)
            return carry

        lax.fori_loop(0, 5, turn, 0)
        relay_home(5)
        for h in range(2):
            edge_arrived(4, h).wait_recv()
            far_arrived(3, h).wait_recv()
            part[4, h] = part[4, h] + land_edge[4, h] + land_far[3, h]
        project(4, 0)
        distribute(0, 3 + side, True)

    @pl.when(mid == 0)
    def _():
        for j in range(3):
            for h in range(2):
                far_arrived(j, h).wait_recv()
                part[5 + j, h] = part[5 + j, h] + land_far[j, h]
            project(5 + j, j)
            if j == 0:
                edge_send(4, 1).wait_send()
            distribute(j, example(5 + j), j == 2)

    owner = [0, 0, 0, 1, 2, 3, 3, 3]
    early = (1, 2, 5, 6)
    for n, i in enumerate(early):
        @pl.when(me != owner[i])
        def _():
            rows_arrived(my_col, i).wait_recv()
            forward(i, n).start()

    for i in range(count):
        if i not in early:
            @pl.when(me != owner[i])
            def _():
                rows_arrived(my_col, i).wait_recv()

    for i in range(count):
        rows_arrived(1 - my_col, i).wait_recv()

    def core_copy(rep):
        block = allp.at[pl.ds(rep * 2 * count, 2 * count)]
        return pltpu.make_async_remote_copy(
            src_ref=block,
            dst_ref=block,
            send_sem=send_core,
            recv_sem=recv_core,
            device_id={"rep": 1 - my_rep},
            device_id_type=MESH,
        )

    def widen(rep):
        first = pl.multiple_of(rep * 2 * count, 2 * count)
        for p in range(block_p):
            rows = allp[pl.ds(first, 2 * count), p, :]
            upper = rows.astype(jnp.bfloat16)
            wide[pl.ds(first, 2 * count), p * SKETCH : (p + 1) * SKETCH] = upper
            lower = (rows - upper.astype(jnp.float32)).astype(jnp.bfloat16)
            wide[pl.ds(4 * count + first, 2 * count), p * SKETCH : (p + 1) * SKETCH] = lower

    core_copy(my_rep).start()
    widen(my_rep)
    core_copy(1 - my_rep).wait_recv()
    widen(1 - my_rep)
    for k in range(gram_parts):
        load_gram(k).wait()

    examples = 4 * count
    per = chunks // HIDDEN

    def sum_send(n, land, recv, m, z):
        return pltpu.make_async_remote_copy(
            src_ref=psum.at[n],
            dst_ref=land.at[m],
            send_sem=send_sum.at[n],
            recv_sem=recv.at[m],
            device_id={"hidden": z},
            device_id_type=MESH,
        )

    def sum_arrived(land, recv, m):
        return pltpu.make_async_remote_copy(
            src_ref=psum.at[0],
            dst_ref=land.at[m],
            send_sem=send_sum.at[0],
            recv_sem=recv.at[m],
            device_id={"rep": 1 - my_rep},
            device_id_type=MESH,
        )

    def gram_step(n, carry):
        d = n // per
        place_d = (HIDDEN - 1 - d) + side * (2 * d - HIDDEN + 1)
        column = pl.multiple_of((place_d * per + lax.rem(n, per)) * step_cols, step_cols)
        both = jnp.dot(wide[...], gram_buf[:, pl.ds(column, step_cols)], preferred_element_type=jnp.float32)
        total = both[:examples] + both[examples:]
        for rep in range(2):
            for col in range(2):
                a, b = (rep * 2 + col) * count, (col * 2 + rep) * count
                psum[n, b : b + count, :] = total[a : a + count]

        @pl.when(jnp.logical_and(mid == 0, n < 3 * per))
        def _():
            sum_send(n, sum_edge, recv_sum_edge, n, own_mid).start()

        @pl.when(jnp.logical_and(mid == 1, n >= 2 * per))
        def _():
            m = n - 2 * per
            sum_arrived(sum_edge, recv_sum_edge, m).wait_recv()
            psum[m] = psum[m] + sum_edge[m]
            sum_send(m, sum_far, recv_sum_far, m, far_mid).start()

        return carry

    lax.fori_loop(0, chunks, gram_step, 0)

    @pl.when(mid == 1)
    def _():
        for m in range(per):
            sum_arrived(sum_far, recv_sum_far, m).wait_recv()
            n = 3 * per + m
            psum[n] = psum[n] + sum_far[m]
            sum_send(n, sum_far, recv_sum_far, m, own_edge).start()
        for m in range(per):
            n = 2 * per + m
            sum_arrived(sum_edge, recv_sum_edge, n).wait_recv()
            sum_arrived(sum_far, recv_sum_far, per + m).wait_recv()
            out_ref[:, m * step_cols : (m + 1) * step_cols] = psum[n] + sum_edge[n] + sum_far[per + m]

    @pl.when(mid == 0)
    def _():
        for m in range(per):
            sum_arrived(sum_far, recv_sum_far, m).wait_recv()
            out_ref[:, m * step_cols : (m + 1) * step_cols] = psum[3 * per + m] + sum_far[m]

    core_copy(my_rep).wait_send()

    @pl.when(mid == 0)
    def _():
        for h in range(2):
            for k in range(5):
                if (k, h) != (4, 1):
                    edge_send(k, h).wait_send()
        for j in range(3):
            for d, c in row_sends(j == 2):
                rows_copy(j, 0, d, c).wait_send()
        for n in range(3 * per):
            sum_send(n, sum_edge, recv_sum_edge, n, own_mid).wait_send()

    @pl.when(mid == 1)
    def _():
        for h in range(2):
            for k in range(4):
                far_send(k, h).wait_send()
            for j in range(3):
                home_send(j, h).wait_send()
        for d, c in row_sends(True):
            rows_copy(0, 0, d, c).wait_send()
        for m in range(2 * per):
            sum_send(m, sum_far, recv_sum_far, m, far_mid).wait_send()
        for m in range(per):
            sum_send(3 * per + m, sum_far, recv_sum_far, m, own_edge).wait_send()

    for n, i in enumerate(early):
        @pl.when(me != owner[i])
        def _():
            forward(i, n).wait_send()


def fused(inputs, grads, in_signs, out_signs, in_rows, out_rows, inv_gram):
    count = inputs.shape[0] // SEQ
    block_p = SKETCH // HIDDEN
    examples = 4 * count
    share = inv_gram.shape[1] // HIDDEN
    chunks = inv_gram.shape[1] // STEP
    f32 = jnp.float32
    dma = pltpu.SemaphoreType.DMA
    vmem = pl.BlockSpec(memory_space=pltpu.VMEM)
    hbm = pl.BlockSpec(memory_space=pl.ANY)
    return pl.pallas_call(
        fused_kernel,
        out_shape=jax.ShapeDtypeStruct((examples, share), f32),
        in_specs=[hbm, hbm, vmem, vmem, vmem, vmem, hbm],
        out_specs=vmem,
        scratch_shapes=[
            pltpu.VMEM((count, SEQ, inputs.shape[1]), jnp.bfloat16),
            pltpu.VMEM((count, SEQ, grads.shape[1]), jnp.bfloat16),
            pltpu.VMEM(inv_gram.shape, jnp.bfloat16),
            pltpu.VMEM((inputs.shape[1], SKETCH), jnp.bfloat16),
            pltpu.VMEM((grads.shape[1], SKETCH), jnp.bfloat16),
            pltpu.VMEM((count, 2, SEQ, SKETCH), f32),
            pltpu.VMEM((5, 2, SEQ, SKETCH), f32),
            pltpu.VMEM((4, 2, SEQ, SKETCH), f32),
            pltpu.VMEM((3, SKETCH, SKETCH), f32),
            pltpu.VMEM((examples, block_p, SKETCH), f32),
            pltpu.VMEM((2 * examples, block_p * SKETCH), jnp.bfloat16),
            pltpu.VMEM((chunks, examples, STEP), f32),
            pltpu.VMEM((3 * chunks // HIDDEN, examples, STEP), f32),
            pltpu.VMEM((2 * chunks // HIDDEN, examples, STEP), f32),
            dma((count,)),
            dma((count,)),
            dma((4,)),
            dma((count, 2)),
            dma((5, 2)),
            dma((4, 2)),
            dma((3, HIDDEN, 2)),
            dma((4,)),
            dma((2, count)),
            dma,
            dma,
            dma((chunks,)),
            dma((3 * chunks // HIDDEN,)),
            dma((2 * chunks // HIDDEN,)),
        ],
        compiler_params=pltpu.CompilerParams(
            collective_id=0, has_side_effects=True, vmem_limit_bytes=63 << 20
        ),
    )(
        inputs,
        grads,
        in_signs.reshape(inputs.shape[1] // LANES, LANES),
        out_signs.reshape(grads.shape[1] // LANES, LANES),
        in_rows.reshape(1, SKETCH),
        out_rows.reshape(1, SKETCH),
        inv_gram,
    )


def plain_sketch(values, signs, rows, width, shard):
    inner = width // HAD
    local_high = values.shape[1] // inner
    high, low = rows // inner, rows % inner
    feature = jnp.arange(values.shape[1], dtype=jnp.int32)
    sources = shard * local_high + feature // inner
    sign = (1 - 2 * had_parity(high[None, :], sources[:, None])) * signs[:, None]
    hit = (feature % inner)[:, None] == low[None, :]
    matrix = jnp.where(hit, sign.astype(jnp.float32) / math.sqrt(HAD), 0.0)
    return jnp.dot(values, matrix.astype(jnp.bfloat16), preferred_element_type=jnp.float32)


def plain(inputs, grads, in_signs, out_signs, in_rows, out_rows, inv_gram):
    shard = lax.axis_index("hidden")
    out_part = plain_sketch(grads, out_signs, out_rows, OUT_W, shard)
    in_part = plain_sketch(inputs, in_signs, in_rows, IN_W, shard)
    block_p = inv_gram.shape[0] // SKETCH
    count = inputs.shape[0] // SEQ
    out_mine = lax.psum_scatter(out_part, "hidden", scatter_dimension=1, tiled=True)
    in_sketch = lax.psum(in_part, "hidden")
    projected = jnp.einsum(
        "esp,esq->epq",
        out_mine.reshape(count, SEQ, block_p),
        in_sketch.reshape(count, SEQ, SKETCH),
        precision=lax.Precision.HIGHEST,
    )
    projected = projected.reshape(count, block_p * SKETCH)
    partial_out = jnp.dot(
        lax.all_gather(projected, ("cols", "rep"), axis=0, tiled=True),
        inv_gram.astype(jnp.float32),
        precision=lax.Precision.HIGHEST,
        preferred_element_type=jnp.float32,
    )
    return lax.psum_scatter(partial_out, "hidden", scatter_dimension=1, tiled=True)


def solution(mesh):
    dims = tuple(mesh.shape[name] for name in ("hidden", "cols", "rep"))

    def on_device(inputs, *rest):
        if dims == (HIDDEN, 2, 2) and inputs.shape[0] == 8 * SEQ:
            return fused(inputs, *rest)
        return plain(inputs, *rest)

    return jax.shard_map(
        on_device,
        mesh=mesh,
        in_specs=(
            P(("groups", "cols", "rep"), "hidden"),
            P(("groups", "cols", "rep"), "hidden"),
            P("hidden"),
            P("hidden"),
            P(),
            P(),
            P("hidden", ("cols", "rep")),
        ),
        out_specs=P("groups", ("cols", "rep", "hidden")),
        check_vma=False,
    )
```

```python
import functools
import math

import jax
import jax.numpy as jnp
from jax import lax
from jax.experimental import pallas as pl
from jax.experimental.pallas import tpu as pltpu
from jax.sharding import PartitionSpec as P

IN_W = 28672
OUT_W = 8192
HAD = 64
SKETCH = 128
SEQ = 128
LANES = 128
HIDDEN = 4
STEP = 512
PIECES = 4
FIRST = 4
LAG = 1
MESH = pl.DeviceIdType.MESH


def had_parity(left, right):
    both = jnp.bitwise_and(left, right)
    for shift in (4, 2, 1):
        both = jnp.bitwise_xor(both, jnp.right_shift(both, shift))
    return jnp.bitwise_and(both, 1)


def split_rows(rows, inner):
    high = jnp.floor((rows.astype(jnp.float32) + 0.5) * (1.0 / inner)).astype(jnp.int32)
    return high, rows - high * inner


def build_matrix(rows_ref, sign_ref, out_ref, shard, width):
    inner = width // HAD
    local_high = out_ref.shape[0] // inner
    high, low = split_rows(rows_ref[...], inner)
    hit = lax.broadcasted_iota(jnp.int32, (inner, SKETCH), 0) == low
    onehot = jnp.where(hit, 1.0, 0.0)
    sign = sign_ref[...].astype(jnp.float32).astype(jnp.bfloat16)
    line = lax.broadcasted_iota(jnp.int32, (sign.shape[0], SKETCH), 0)
    lane = lax.broadcasted_iota(jnp.int32, (LANES, SKETCH), 0)
    picked = {}
    for h in range(local_high):
        first, offset = divmod(h * inner, LANES)
        at = offset + low
        if offset not in picked:
            pick = jnp.where(lane == jnp.bitwise_and(at, LANES - 1), 1.0, 0.0).astype(jnp.bfloat16)
            picked[offset] = jnp.dot(sign, pick, preferred_element_type=jnp.float32)
        own = line == first + jnp.right_shift(at, LANES.bit_length() - 1)
        coef = jnp.sum(jnp.where(own, picked[offset], 0.0), axis=0, keepdims=True)
        parity = had_parity(high, shard * local_high + h)
        coef = coef * (1 - 2 * parity).astype(jnp.float32) * (1.0 / math.sqrt(HAD))
        out_ref[h * inner : (h + 1) * inner, :] = (onehot * coef).astype(jnp.bfloat16)


def fused_kernel(
    x_ref,
    g_ref,
    in_sign_ref,
    out_sign_ref,
    in_rows_ref,
    out_rows_ref,
    gram_ref,
    out_ref,
    in_sign,
    out_sign,
    in_rows,
    out_rows,
    small_sem,
    x_buf,
    g_buf,
    gram_buf,
    mat_in,
    mat_out,
    part,
    land_edge,
    land_far,
    proj,
    allp,
    wide,
    psum,
    sum_land,
    x_sem,
    g_sem,
    gram_sem,
    send_part,
    recv_edge,
    recv_far,
    send_rows,
    send_fwd,
    recv_rows,
    send_core,
    recv_core,
    send_sum,
    recv_sum,
):
    me = lax.axis_index("hidden")
    my_col = lax.axis_index("cols")
    my_rep = lax.axis_index("rep")
    count = x_buf.shape[0]
    side = me // 2
    mid = lax.rem((me + 1) // 2, 2)
    own_edge, own_mid, far_mid = 3 * side, 1 + side, 2 - side
    block_p = SKETCH // HIDDEN
    chunks = psum.shape[0]
    step_cols = psum.shape[2]

    def example(k):
        early = 1 - (k + count - 3) // count
        label = count - 1 - k + early * (2 * k - 2)
        return label + side * (count - 1 - 2 * label)

    def load_x(k):
        row = pl.multiple_of(example(k) * SEQ, SEQ)
        return pltpu.make_async_copy(x_ref.at[pl.ds(row, SEQ)], x_buf.at[k], x_sem.at[k])

    def load_g(k):
        row = pl.multiple_of(example(k) * SEQ, SEQ)
        return pltpu.make_async_copy(g_ref.at[pl.ds(row, SEQ)], g_buf.at[k], g_sem.at[k])

    gram_parts = gram_sem.shape[0]
    gram_rows = gram_ref.shape[0] // gram_parts

    def load_gram(k):
        where = pl.ds(k * gram_rows, gram_rows)
        return pltpu.make_async_copy(gram_ref.at[where], gram_buf.at[where], gram_sem.at[k])

    small = [(out_rows_ref, out_rows), (out_sign_ref, out_sign), (in_rows_ref, in_rows), (in_sign_ref, in_sign)]
    loads = [pltpu.make_async_copy(far, near, small_sem.at[n]) for n, (far, near) in enumerate(small)]
    for load in loads:
        load.start()
    load_g(0).start()
    load_x(0).start()

    barrier = pltpu.get_barrier_semaphore()
    pl.semaphore_signal(barrier, inc=1, device_id={"rep": 1 - my_rep}, device_id_type=MESH)
    for d in range(1, HIDDEN):
        pl.semaphore_signal(barrier, inc=1, device_id={"hidden": lax.rem(me + d, HIDDEN)}, device_id_type=MESH)
    for d in range(HIDDEN):
        pl.semaphore_signal(
            barrier, inc=1, device_id={"hidden": lax.rem(me + d, HIDDEN), "cols": 1 - my_col}, device_id_type=MESH
        )
    for load in loads:
        load.wait()
    for k in range(1, count):
        load_g(k).start()
        load_x(k).start()
    build_matrix(out_rows, out_sign, mat_out, me, OUT_W)
    build_matrix(in_rows, in_sign, mat_in, me, IN_W)

    pieces = send_part.shape[1]
    piece = 2 * SEQ // pieces

    def cut(ref, k, c):
        row = pl.multiple_of(lax.rem(c, pieces // 2) * piece, piece)
        return ref.at[k, c // (pieces // 2), pl.ds(row, piece)]

    def edge_send(k, c):
        return pltpu.make_async_remote_copy(
            src_ref=cut(part, k, c),
            dst_ref=cut(land_edge, k, c),
            send_sem=send_part.at[k, c],
            recv_sem=recv_edge.at[k, c],
            device_id={"hidden": own_mid},
            device_id_type=MESH,
        )

    def far_send(k, c):
        return pltpu.make_async_remote_copy(
            src_ref=cut(part, k, c),
            dst_ref=cut(land_far, k, c),
            send_sem=send_part.at[k, c],
            recv_sem=recv_far.at[k, c],
            device_id={"hidden": far_mid},
            device_id_type=MESH,
        )

    def home_send(j, c):
        return pltpu.make_async_remote_copy(
            src_ref=cut(part, 5 + j, c),
            dst_ref=cut(land_far, j, c),
            send_sem=send_part.at[5 + j, c],
            recv_sem=recv_far.at[j, c],
            device_id={"hidden": own_edge},
            device_id_type=MESH,
        )

    def edge_arrived(k, c):
        return pltpu.make_async_remote_copy(
            src_ref=cut(part, k, c),
            dst_ref=cut(land_edge, k, c),
            send_sem=send_part.at[k, c],
            recv_sem=recv_edge.at[k, c],
            device_id={"rep": 1 - my_rep},
            device_id_type=MESH,
        )

    def far_arrived(k, c):
        return pltpu.make_async_remote_copy(
            src_ref=cut(part, k, c),
            dst_ref=cut(land_far, k, c),
            send_sem=send_part.at[k, c],
            recv_sem=recv_far.at[k, c],
            device_id={"rep": 1 - my_rep},
            device_id_type=MESH,
        )

    def add(k, c, landed):
        here = cut(part, k, c)
        here[...] = here[...] + landed[...]

    def relay_edge(n):
        k, c = n // pieces, lax.rem(n, pieces)
        edge_arrived(k, c).wait_recv()
        add(k, c, cut(land_edge, k, c))
        far_send(k, c).start()

    def relay_home(n):
        j, c = n // pieces, lax.rem(n, pieces)
        far_arrived(j, c).wait_recv()
        add(5 + j, c, cut(land_far, j, c))
        home_send(j, c).start()

    def sketch_step(k, carry):
        sends = jnp.logical_and(mid == 0, k < 5)
        load_g(k).wait()
        part[k, 0] = jnp.dot(g_buf[k], mat_out[...], preferred_element_type=jnp.float32)

        @pl.when(k == 0)
        def _():
            pl.semaphore_wait(barrier, 2 * HIDDEN)

        @pl.when(sends)
        def _():
            for c in range(pieces // 2):
                edge_send(k, c).start()

        load_x(k).wait()
        part[k, 1] = jnp.dot(x_buf[k], mat_in[...], preferred_element_type=jnp.float32)

        @pl.when(sends)
        def _():
            for c in range(pieces // 2, pieces):
                edge_send(k, c).start()

        @pl.when(jnp.logical_and(mid == 1, k >= count - FIRST))
        def _():
            relay_edge(k - count + FIRST)

        return carry

    lax.fori_loop(0, count, sketch_step, 0)
    for k in range(gram_parts):
        load_gram(k).start()

    def project(k, slot):
        proj[slot] = lax.dot_general(
            part[k, 0],
            part[k, 1],
            (((0,), (0,)), ((), ())),
            precision=lax.Precision.HIGHEST,
            preferred_element_type=jnp.float32,
        )

    def place(rep, col, i):
        return (rep * 2 + col) * count + i

    def rows_copy(slot, i, d, c):
        z = lax.rem(me + d, HIDDEN)
        col = my_col + c * (1 - 2 * my_col)
        return pltpu.make_async_remote_copy(
            src_ref=proj.at[slot, pl.ds(pl.multiple_of(z * block_p, block_p), block_p), :],
            dst_ref=allp.at[place(my_rep, my_col, i)],
            send_sem=send_rows.at[slot, d, c],
            recv_sem=recv_rows.at[my_col, i],
            device_id={"hidden": z, "cols": col},
            device_id_type=MESH,
        )

    def forward(i, n):
        block = allp.at[place(my_rep, my_col, i)]
        return pltpu.make_async_remote_copy(
            src_ref=block,
            dst_ref=block,
            send_sem=send_fwd.at[n],
            recv_sem=recv_rows.at[my_col, i],
            device_id={"cols": 1 - my_col},
            device_id_type=MESH,
        )

    def rows_arrived(col, i):
        block = allp.at[place(my_rep, col, i)]
        return pltpu.make_async_remote_copy(
            src_ref=block,
            dst_ref=block,
            send_sem=send_fwd.at[0],
            recv_sem=recv_rows.at[col, i],
            device_id={"cols": 1 - my_col},
            device_id_type=MESH,
        )

    def row_sends(late):
        both = [(d, c) for d in range(HIDDEN) for c in range(2) if (d, c) != (0, 0)]
        return both if late else [(d, c) for d, c in both if d == 0 or c == 0]

    def distribute(slot, i, late):
        for d, c in row_sends(late):
            rows_copy(slot, i, d, c).start()
        allp[place(my_rep, my_col, i)] = proj[slot, pl.ds(pl.multiple_of(me * block_p, block_p), block_p), :]

    @pl.when(mid == 1)
    def _():
        def turn(n, carry):
            relay_edge(n + FIRST)

            @pl.when(n >= LAG)
            def _():
                relay_home(n - LAG)

            return carry

        lax.fori_loop(0, 4 * pieces - FIRST, turn, 0)

        def rest(n, carry):
            relay_home(n)
            return carry

        lax.fori_loop(4 * pieces - FIRST - LAG, 3 * pieces, rest, 0)
        for c in range(pieces):
            edge_arrived(4, c).wait_recv()
            far_arrived(3, c).wait_recv()
            add(4, c, cut(land_edge, 4, c))
            add(4, c, cut(land_far, 3, c))
        project(4, 0)
        distribute(0, 3 + side, True)

    @pl.when(mid == 0)
    def _():
        for j in range(3):
            for c in range(pieces):
                far_arrived(j, c).wait_recv()
                add(5 + j, c, cut(land_far, j, c))
            project(5 + j, j)
            if j == 0:
                edge_send(4, pieces - 1).wait_send()
            distribute(j, example(5 + j), j == 2)

    owner = [0, 0, 0, 1, 2, 3, 3, 3]
    early = (1, 2, 5, 6)
    for n, i in enumerate(early):
        @pl.when(me != owner[i])
        def _():
            rows_arrived(my_col, i).wait_recv()
            forward(i, n).start()

    for i in range(count):
        if i not in early:
            @pl.when(me != owner[i])
            def _():
                rows_arrived(my_col, i).wait_recv()

    for i in range(count):
        rows_arrived(1 - my_col, i).wait_recv()

    def core_copy(rep):
        block = allp.at[pl.ds(rep * 2 * count, 2 * count)]
        return pltpu.make_async_remote_copy(
            src_ref=block,
            dst_ref=block,
            send_sem=send_core,
            recv_sem=recv_core,
            device_id={"rep": 1 - my_rep},
            device_id_type=MESH,
        )

    def widen(rep):
        first = pl.multiple_of(rep * 2 * count, 2 * count)
        for p in range(block_p):
            rows = allp[pl.ds(first, 2 * count), p, :]
            upper = rows.astype(jnp.bfloat16)
            wide[pl.ds(first, 2 * count), p * SKETCH : (p + 1) * SKETCH] = upper
            lower = (rows - upper.astype(jnp.float32)).astype(jnp.bfloat16)
            wide[pl.ds(4 * count + first, 2 * count), p * SKETCH : (p + 1) * SKETCH] = lower

    core_copy(my_rep).start()
    widen(my_rep)
    core_copy(1 - my_rep).wait_recv()
    widen(1 - my_rep)
    for k in range(gram_parts):
        load_gram(k).wait()

    examples = 4 * count
    per = chunks // HIDDEN

    def sum_send(n, m, z):
        return pltpu.make_async_remote_copy(
            src_ref=psum.at[n],
            dst_ref=sum_land.at[m],
            send_sem=send_sum.at[n],
            recv_sem=recv_sum.at[m],
            device_id={"hidden": z},
            device_id_type=MESH,
        )

    def sum_arrived(m):
        return pltpu.make_async_remote_copy(
            src_ref=psum.at[0],
            dst_ref=sum_land.at[m],
            send_sem=send_sum.at[0],
            recv_sem=recv_sum.at[m],
            device_id={"rep": 1 - my_rep},
            device_id_type=MESH,
        )

    def kind(d, value):
        return 1 - (lax.rem(d + HIDDEN - value, HIDDEN) + HIDDEN - 1) // HIDDEN

    far_edge, neighbour = 3 - 3 * side, own_edge + own_mid - me

    def gram_step(n, carry):
        d = n // per
        place_d = kind(d, 0) * far_mid + kind(d, 1) * far_edge + kind(d, 2) * neighbour + kind(d, 3) * me
        column = pl.multiple_of((place_d * per + lax.rem(n, per)) * step_cols, step_cols)
        both = jnp.dot(wide[...], gram_buf[:, pl.ds(column, step_cols)], preferred_element_type=jnp.float32)
        total = both[:examples] + both[examples:]
        for rep in range(2):
            for col in range(2):
                a, b = (rep * 2 + col) * count, (col * 2 + rep) * count
                psum[n, b : b + count, :] = total[a : a + count]

        @pl.when(jnp.logical_and(mid == 0, n < per))
        def _():
            sum_send(n, n, own_mid).start()

        @pl.when(jnp.logical_and(n >= per, n < 2 * per))
        def _():
            sum_send(n, (1 - mid) * per + n, far_edge).start()

        @pl.when(jnp.logical_and(n >= 2 * per, n < 3 * per))
        def _():
            sum_send(n, n - (1 + mid) * per, neighbour).start()

        @pl.when(jnp.logical_and(mid == 1, jnp.logical_and(n >= 2 * per, n < 3 * per)))
        def _():
            m = n - 2 * per
            sum_arrived(m).wait_recv()
            psum[m] = psum[m] + sum_land[m]
            sum_send(m, 2 * per + m, far_mid).start()

        return carry

    lax.fori_loop(0, chunks, gram_step, 0)

    for m in range(per):
        @pl.when(mid == 0)
        def _():
            sum_arrived(m).wait_recv()
            psum[3 * per + m] = psum[3 * per + m] + sum_land[m]

        sum_arrived(2 * per + m).wait_recv()
        sum_arrived(per + m).wait_recv()
        out_ref[:, m * step_cols : (m + 1) * step_cols] = psum[3 * per + m] + sum_land[2 * per + m] + sum_land[per + m]

    core_copy(my_rep).wait_send()

    @pl.when(mid == 0)
    def _():
        for c in range(pieces):
            for k in range(5):
                if (k, c) != (4, pieces - 1):
                    edge_send(k, c).wait_send()
        for j in range(3):
            for d, c in row_sends(j == 2):
                rows_copy(j, 0, d, c).wait_send()

    @pl.when(mid == 1)
    def _():
        for c in range(pieces):
            for k in range(4):
                far_send(k, c).wait_send()
            for j in range(3):
                home_send(j, c).wait_send()
        for d, c in row_sends(True):
            rows_copy(0, 0, d, c).wait_send()

    for n in range(3 * per):
        sum_send(n, 0, neighbour).wait_send()

    for n, i in enumerate(early):
        @pl.when(me != owner[i])
        def _():
            forward(i, n).wait_send()


def fused(inputs, grads, in_signs, out_signs, in_rows, out_rows, inv_gram):
    count = inputs.shape[0] // SEQ
    block_p = SKETCH // HIDDEN
    examples = 4 * count
    share = inv_gram.shape[1] // HIDDEN
    chunks = inv_gram.shape[1] // STEP
    f32 = jnp.float32
    dma = pltpu.SemaphoreType.DMA
    vmem = pl.BlockSpec(memory_space=pltpu.VMEM)
    hbm = pl.BlockSpec(memory_space=pl.ANY)
    return pl.pallas_call(
        fused_kernel,
        out_shape=pltpu.VMEM((examples, share), f32),
        in_specs=[hbm] * 7,
        out_specs=vmem,
        scratch_shapes=[
            pltpu.VMEM((inputs.shape[1] // LANES, LANES), jnp.int32),
            pltpu.VMEM((grads.shape[1] // LANES, LANES), jnp.int32),
            pltpu.VMEM((1, SKETCH), jnp.int32),
            pltpu.VMEM((1, SKETCH), jnp.int32),
            dma((4,)),
            pltpu.VMEM((count, SEQ, inputs.shape[1]), jnp.bfloat16),
            pltpu.VMEM((count, SEQ, grads.shape[1]), jnp.bfloat16),
            pltpu.VMEM(inv_gram.shape, jnp.bfloat16),
            pltpu.VMEM((inputs.shape[1], SKETCH), jnp.bfloat16),
            pltpu.VMEM((grads.shape[1], SKETCH), jnp.bfloat16),
            pltpu.VMEM((count, 2, SEQ, SKETCH), f32),
            pltpu.VMEM((5, 2, SEQ, SKETCH), f32),
            pltpu.VMEM((4, 2, SEQ, SKETCH), f32),
            pltpu.VMEM((3, SKETCH, SKETCH), f32),
            pltpu.VMEM((examples, block_p, SKETCH), f32),
            pltpu.VMEM((2 * examples, block_p * SKETCH), jnp.bfloat16),
            pltpu.VMEM((chunks, examples, STEP), f32),
            pltpu.VMEM((3 * chunks // HIDDEN, examples, STEP), f32),
            dma((count,)),
            dma((count,)),
            dma((4,)),
            dma((count, PIECES)),
            dma((5, PIECES)),
            dma((4, PIECES)),
            dma((3, HIDDEN, 2)),
            dma((4,)),
            dma((2, count)),
            dma,
            dma,
            dma((chunks,)),
            dma((3 * chunks // HIDDEN,)),
        ],
        compiler_params=pltpu.CompilerParams(
            collective_id=0, has_side_effects=True, vmem_limit_bytes=63 << 20
        ),
    )(
        inputs,
        grads,
        in_signs.reshape(inputs.shape[1] // LANES, LANES),
        out_signs.reshape(grads.shape[1] // LANES, LANES),
        in_rows.reshape(1, SKETCH),
        out_rows.reshape(1, SKETCH),
        inv_gram,
    )


def plain_sketch(values, signs, rows, width, shard):
    inner = width // HAD
    local_high = values.shape[1] // inner
    high, low = rows // inner, rows % inner
    feature = jnp.arange(values.shape[1], dtype=jnp.int32)
    sources = shard * local_high + feature // inner
    sign = (1 - 2 * had_parity(high[None, :], sources[:, None])) * signs[:, None]
    hit = (feature % inner)[:, None] == low[None, :]
    matrix = jnp.where(hit, sign.astype(jnp.float32) / math.sqrt(HAD), 0.0)
    return jnp.dot(values, matrix.astype(jnp.bfloat16), preferred_element_type=jnp.float32)


def plain(inputs, grads, in_signs, out_signs, in_rows, out_rows, inv_gram):
    shard = lax.axis_index("hidden")
    out_part = plain_sketch(grads, out_signs, out_rows, OUT_W, shard)
    in_part = plain_sketch(inputs, in_signs, in_rows, IN_W, shard)
    block_p = inv_gram.shape[0] // SKETCH
    count = inputs.shape[0] // SEQ
    out_mine = lax.psum_scatter(out_part, "hidden", scatter_dimension=1, tiled=True)
    in_sketch = lax.psum(in_part, "hidden")
    projected = jnp.einsum(
        "esp,esq->epq",
        out_mine.reshape(count, SEQ, block_p),
        in_sketch.reshape(count, SEQ, SKETCH),
        precision=lax.Precision.HIGHEST,
    )
    projected = projected.reshape(count, block_p * SKETCH)
    partial_out = jnp.dot(
        lax.all_gather(projected, ("cols", "rep"), axis=0, tiled=True),
        inv_gram.astype(jnp.float32),
        precision=lax.Precision.HIGHEST,
        preferred_element_type=jnp.float32,
    )
    return lax.psum_scatter(partial_out, "hidden", scatter_dimension=1, tiled=True)


def solution(mesh):
    dims = tuple(mesh.shape[name] for name in ("hidden", "cols", "rep"))

    def on_device(inputs, *rest):
        if dims == (HIDDEN, 2, 2) and inputs.shape[0] == 8 * SEQ:
            return fused(inputs, *rest)
        return plain(inputs, *rest)

    return jax.shard_map(
        on_device,
        mesh=mesh,
        in_specs=(
            P(("groups", "cols", "rep"), "hidden"),
            P(("groups", "cols", "rep"), "hidden"),
            P("hidden"),
            P("hidden"),
            P(),
            P(),
            P("hidden", ("cols", "rep")),
        ),
        out_specs=P("groups", ("cols", "rep", "hidden")),
        check_vma=False,
    )
```

```python
import functools
import math

import jax
import jax.numpy as jnp
from jax import lax
from jax.experimental import pallas as pl
from jax.experimental.pallas import tpu as pltpu
from jax.sharding import PartitionSpec as P

IN_W = 28672
OUT_W = 8192
HAD = 64
SKETCH = 128
SEQ = 128
LANES = 128
HIDDEN = 4
STEP = 512
PIECES = 4
LAG = 5
MESH = pl.DeviceIdType.MESH


def had_parity(left, right):
    both = jnp.bitwise_and(left, right)
    for shift in (4, 2, 1):
        both = jnp.bitwise_xor(both, jnp.right_shift(both, shift))
    return jnp.bitwise_and(both, 1)


def split_rows(rows, inner):
    high = jnp.floor((rows.astype(jnp.float32) + 0.5) * (1.0 / inner)).astype(jnp.int32)
    return high, rows - high * inner


def build_matrix(rows_ref, sign_ref, out_ref, shard, width):
    inner = width // HAD
    local_high = out_ref.shape[0] // inner
    high, low = split_rows(rows_ref[...], inner)
    hit = lax.broadcasted_iota(jnp.int32, (inner, SKETCH), 0) == low
    onehot = jnp.where(hit, 1.0, 0.0)
    sign = sign_ref[...].astype(jnp.float32).astype(jnp.bfloat16)
    line = lax.broadcasted_iota(jnp.int32, (sign.shape[0], SKETCH), 0)
    lane = lax.broadcasted_iota(jnp.int32, (LANES, SKETCH), 0)
    picked = {}
    for h in range(local_high):
        first, offset = divmod(h * inner, LANES)
        at = offset + low
        if offset not in picked:
            pick = jnp.where(lane == jnp.bitwise_and(at, LANES - 1), 1.0, 0.0).astype(jnp.bfloat16)
            picked[offset] = jnp.dot(sign, pick, preferred_element_type=jnp.float32)
        own = line == first + jnp.right_shift(at, LANES.bit_length() - 1)
        coef = jnp.sum(jnp.where(own, picked[offset], 0.0), axis=0, keepdims=True)
        parity = had_parity(high, shard * local_high + h)
        coef = coef * (1 - 2 * parity).astype(jnp.float32) * (1.0 / math.sqrt(HAD))
        out_ref[h * inner : (h + 1) * inner, :] = (onehot * coef).astype(jnp.bfloat16)


def fused_kernel(
    x_ref,
    g_ref,
    in_sign_ref,
    out_sign_ref,
    in_rows_ref,
    out_rows_ref,
    gram_ref,
    out_ref,
    in_sign,
    out_sign,
    in_rows,
    out_rows,
    small_sem,
    x_buf,
    g_buf,
    gram_buf,
    mat_in,
    mat_out,
    part,
    land_edge,
    land_far,
    proj,
    allp,
    wide,
    psum,
    sum_land,
    x_sem,
    g_sem,
    gram_sem,
    send_part,
    recv_edge,
    recv_far,
    send_rows,
    send_fwd,
    recv_rows,
    send_core,
    recv_core,
    send_sum,
    recv_sum,
):
    me = lax.axis_index("hidden")
    my_col = lax.axis_index("cols")
    my_rep = lax.axis_index("rep")
    count = x_buf.shape[0]
    side = me // 2
    mid = lax.rem((me + 1) // 2, 2)
    own_edge, own_mid, far_mid = 3 * side, 1 + side, 2 - side
    block_p = SKETCH // HIDDEN
    chunks = psum.shape[0]
    step_cols = psum.shape[2]

    def example(k):
        early = 1 - (k + count - 3) // count
        label = count - 1 - k + early * (2 * k - 2)
        return label + side * (count - 1 - 2 * label)

    def load_x(k):
        row = pl.multiple_of(example(k) * SEQ, SEQ)
        return pltpu.make_async_copy(x_ref.at[pl.ds(row, SEQ)], x_buf.at[k], x_sem.at[k])

    def load_g(k):
        row = pl.multiple_of(example(k) * SEQ, SEQ)
        return pltpu.make_async_copy(g_ref.at[pl.ds(row, SEQ)], g_buf.at[k], g_sem.at[k])

    gram_parts = gram_sem.shape[0]
    gram_rows = gram_ref.shape[0] // gram_parts

    def load_gram(k):
        where = pl.ds(k * gram_rows, gram_rows)
        return pltpu.make_async_copy(gram_ref.at[where], gram_buf.at[where], gram_sem.at[k])

    small = [(out_rows_ref, out_rows), (out_sign_ref, out_sign), (in_rows_ref, in_rows), (in_sign_ref, in_sign)]
    loads = [pltpu.make_async_copy(far, near, small_sem.at[n]) for n, (far, near) in enumerate(small)]
    for load in loads:
        load.start()
    load_g(0).start()
    load_x(0).start()

    barrier = pltpu.get_barrier_semaphore()
    pl.semaphore_signal(barrier, inc=1, device_id={"rep": 1 - my_rep}, device_id_type=MESH)
    for d in range(1, HIDDEN):
        pl.semaphore_signal(barrier, inc=1, device_id={"hidden": lax.rem(me + d, HIDDEN)}, device_id_type=MESH)
    for d in range(HIDDEN):
        pl.semaphore_signal(
            barrier, inc=1, device_id={"hidden": lax.rem(me + d, HIDDEN), "cols": 1 - my_col}, device_id_type=MESH
        )
    for load in loads:
        load.wait()
    for k in range(1, count):
        load_g(k).start()
        load_x(k).start()
    build_matrix(out_rows, out_sign, mat_out, me, OUT_W)
    build_matrix(in_rows, in_sign, mat_in, me, IN_W)

    pieces = send_part.shape[1]
    piece = 2 * SEQ // pieces

    def cut(ref, k, c):
        row = pl.multiple_of(lax.rem(c, pieces // 2) * piece, piece)
        return ref.at[k, c // (pieces // 2), pl.ds(row, piece)]

    def edge_send(k, c):
        return pltpu.make_async_remote_copy(
            src_ref=cut(part, k, c),
            dst_ref=cut(land_edge, k, c),
            send_sem=send_part.at[k, c],
            recv_sem=recv_edge.at[k, c],
            device_id={"hidden": own_mid},
            device_id_type=MESH,
        )

    def far_send(k, c):
        return pltpu.make_async_remote_copy(
            src_ref=cut(part, k, c),
            dst_ref=cut(land_far, k, c),
            send_sem=send_part.at[k, c],
            recv_sem=recv_far.at[k, c],
            device_id={"hidden": far_mid},
            device_id_type=MESH,
        )

    def home_send(j, c):
        return pltpu.make_async_remote_copy(
            src_ref=cut(part, 5 + j, c),
            dst_ref=cut(land_far, j, c),
            send_sem=send_part.at[5 + j, c],
            recv_sem=recv_far.at[j, c],
            device_id={"hidden": own_edge},
            device_id_type=MESH,
        )

    def edge_arrived(k, c):
        return pltpu.make_async_remote_copy(
            src_ref=cut(part, k, c),
            dst_ref=cut(land_edge, k, c),
            send_sem=send_part.at[k, c],
            recv_sem=recv_edge.at[k, c],
            device_id={"rep": 1 - my_rep},
            device_id_type=MESH,
        )

    def far_arrived(k, c):
        return pltpu.make_async_remote_copy(
            src_ref=cut(part, k, c),
            dst_ref=cut(land_far, k, c),
            send_sem=send_part.at[k, c],
            recv_sem=recv_far.at[k, c],
            device_id={"rep": 1 - my_rep},
            device_id_type=MESH,
        )

    def add(k, c, landed):
        here = cut(part, k, c)
        here[...] = here[...] + landed[...]

    def relay_edge(n):
        k, c = n // pieces, lax.rem(n, pieces)
        edge_arrived(k, c).wait_recv()
        add(k, c, cut(land_edge, k, c))
        far_send(k, c).start()

    def relay_home(n):
        j, c = n // pieces, lax.rem(n, pieces)
        far_arrived(j, c).wait_recv()
        add(5 + j, c, cut(land_far, j, c))
        home_send(j, c).start()

    def turn(n):
        relay_edge(n)

        @pl.when(n >= LAG)
        def _():
            relay_home(n - LAG)

    def sketch_step(k, carry):
        sends = jnp.logical_and(mid == 0, k < 5)
        load_g(k).wait()
        part[k, 0] = jnp.dot(g_buf[k], mat_out[...], preferred_element_type=jnp.float32)

        @pl.when(k == 3 * mid)
        def _():
            pl.semaphore_wait(barrier, 2 * HIDDEN)

        @pl.when(sends)
        def _():
            for c in range(pieces // 2):
                edge_send(k, c).start()

        load_x(k).wait()
        part[k, 1] = jnp.dot(x_buf[k], mat_in[...], preferred_element_type=jnp.float32)

        @pl.when(sends)
        def _():
            for c in range(pieces // 2, pieces):
                edge_send(k, c).start()

        @pl.when(jnp.logical_and(mid == 1, k >= 3))
        def _():
            for n in range(2):
                turn(2 * (k - 3) + n)

        return carry

    lax.fori_loop(0, count, sketch_step, 0)
    for k in range(gram_parts):
        load_gram(k).start()

    def split(value):
        upper = value.astype(jnp.bfloat16)
        return upper, (value - upper.astype(jnp.float32)).astype(jnp.bfloat16)

    def project(k, slot):
        left, left_low = split(part[k, 0])
        right, right_low = split(part[k, 1])
        proj[slot] = lax.dot_general(
            jnp.concatenate([left, left, left_low]),
            jnp.concatenate([right, right_low, right]),
            (((0,), (0,)), ((), ())),
            preferred_element_type=jnp.float32,
        )

    def place(rep, col, i):
        return (rep * 2 + col) * count + i

    def rows_copy(slot, i, d, c):
        z = (me, 3 - 3 * side, far_mid, own_edge + own_mid - me)[d]
        col = my_col + c * (1 - 2 * my_col)
        return pltpu.make_async_remote_copy(
            src_ref=proj.at[slot, pl.ds(pl.multiple_of(z * block_p, block_p), block_p), :],
            dst_ref=allp.at[place(my_rep, my_col, i)],
            send_sem=send_rows.at[slot, d, c],
            recv_sem=recv_rows.at[my_col, i],
            device_id={"hidden": z, "cols": col},
            device_id_type=MESH,
        )

    def forward(i, n):
        block = allp.at[place(my_rep, my_col, i)]
        return pltpu.make_async_remote_copy(
            src_ref=block,
            dst_ref=block,
            send_sem=send_fwd.at[n],
            recv_sem=recv_rows.at[my_col, i],
            device_id={"cols": 1 - my_col},
            device_id_type=MESH,
        )

    def rows_arrived(col, i):
        block = allp.at[place(my_rep, col, i)]
        return pltpu.make_async_remote_copy(
            src_ref=block,
            dst_ref=block,
            send_sem=send_fwd.at[0],
            recv_sem=recv_rows.at[col, i],
            device_id={"cols": 1 - my_col},
            device_id_type=MESH,
        )

    def row_sends(late):
        both = [(d, c) for d in (1, 2, 3, 0) for c in (1, 0) if (d, c) != (0, 0)]
        return both if late else [(d, c) for d, c in both if d == 0 or c == 0]

    def distribute(slot, i, late):
        for d, c in row_sends(late):
            rows_copy(slot, i, d, c).start()
        allp[place(my_rep, my_col, i)] = proj[slot, pl.ds(pl.multiple_of(me * block_p, block_p), block_p), :]

    @pl.when(mid == 1)
    def _():
        def later(n, carry):
            turn(n)
            return carry

        lax.fori_loop(2 * (count - 3), 4 * pieces, later, 0)

        def rest(n, carry):
            relay_home(n)
            return carry

        lax.fori_loop(4 * pieces - LAG, 3 * pieces, rest, 0)
        for c in range(pieces):
            edge_arrived(4, c).wait_recv()
            far_arrived(3, c).wait_recv()
            add(4, c, cut(land_edge, 4, c))
            add(4, c, cut(land_far, 3, c))
        project(4, 0)
        distribute(0, 3 + side, True)

    @pl.when(mid == 0)
    def _():
        for j in range(3):
            for c in range(pieces):
                far_arrived(j, c).wait_recv()
                add(5 + j, c, cut(land_far, j, c))
            project(5 + j, j)
            if j == 0:
                edge_send(4, pieces - 1).wait_send()
            distribute(j, example(5 + j), j == 2)

    owner = [0, 0, 0, 1, 2, 3, 3, 3]
    early = (1, 2, 5, 6)
    for n, i in enumerate(early):
        @pl.when(me != owner[i])
        def _():
            rows_arrived(my_col, i).wait_recv()
            forward(i, n).start()

    for i in range(count):
        if i not in early:
            @pl.when(me != owner[i])
            def _():
                rows_arrived(my_col, i).wait_recv()

    for i in range(count):
        rows_arrived(1 - my_col, i).wait_recv()

    def core_copy(rep):
        block = allp.at[pl.ds(rep * 2 * count, 2 * count)]
        return pltpu.make_async_remote_copy(
            src_ref=block,
            dst_ref=block,
            send_sem=send_core,
            recv_sem=recv_core,
            device_id={"rep": 1 - my_rep},
            device_id_type=MESH,
        )

    def widen(rep):
        first = pl.multiple_of(rep * 2 * count, 2 * count)
        for p in range(block_p):
            rows = allp[pl.ds(first, 2 * count), p, :]
            upper = rows.astype(jnp.bfloat16)
            wide[pl.ds(first, 2 * count), p * SKETCH : (p + 1) * SKETCH] = upper
            lower = (rows - upper.astype(jnp.float32)).astype(jnp.bfloat16)
            wide[pl.ds(4 * count + first, 2 * count), p * SKETCH : (p + 1) * SKETCH] = lower

    core_copy(my_rep).start()
    widen(my_rep)
    core_copy(1 - my_rep).wait_recv()
    widen(1 - my_rep)
    for k in range(gram_parts):
        load_gram(k).wait()

    examples = 4 * count
    per = chunks // HIDDEN

    def sum_send(n, m, z):
        return pltpu.make_async_remote_copy(
            src_ref=psum.at[n],
            dst_ref=sum_land.at[m],
            send_sem=send_sum.at[n],
            recv_sem=recv_sum.at[m],
            device_id={"hidden": z},
            device_id_type=MESH,
        )

    def sum_arrived(m):
        return pltpu.make_async_remote_copy(
            src_ref=psum.at[0],
            dst_ref=sum_land.at[m],
            send_sem=send_sum.at[0],
            recv_sem=recv_sum.at[m],
            device_id={"rep": 1 - my_rep},
            device_id_type=MESH,
        )

    def kind(d, value):
        return 1 - (lax.rem(d + HIDDEN - value, HIDDEN) + HIDDEN - 1) // HIDDEN

    far_edge, neighbour = 3 - 3 * side, own_edge + own_mid - me

    def gram_step(n, carry):
        d = n // per
        place_d = kind(d, mid * 2) * far_mid + kind(d, 1 - mid) * far_edge + kind(d, 2 - mid) * neighbour + kind(d, 3) * me
        column = pl.multiple_of((place_d * per + lax.rem(n, per)) * step_cols, step_cols)
        both = jnp.dot(wide[...], gram_buf[:, pl.ds(column, step_cols)], preferred_element_type=jnp.float32)
        total = both[:examples] + both[examples:]
        for rep in range(2):
            for col in range(2):
                a, b = (rep * 2 + col) * count, (col * 2 + rep) * count
                psum[n, b : b + count, :] = total[a : a + count]

        m = lax.rem(n, per)

        @pl.when(jnp.logical_and(mid == 0, d == 0))
        def _():
            sum_send(n, m, own_mid).start()

        @pl.when(d == 1 - mid)
        def _():
            sum_send(n, (2 - mid) * per + m, far_edge).start()

        @pl.when(d == 2 - mid)
        def _():
            sum_send(n, (1 - mid) * per + m, neighbour).start()

        @pl.when(jnp.logical_and(mid == 1, d == 2))
        def _():
            sum_arrived(m).wait_recv()
            psum[n] = psum[n] + sum_land[m]
            sum_send(n, 2 * per + m, far_mid).start()

        return carry

    lax.fori_loop(0, chunks, gram_step, 0)

    for m in range(per):
        @pl.when(mid == 0)
        def _():
            sum_arrived(m).wait_recv()
            psum[3 * per + m] = psum[3 * per + m] + sum_land[m]

        sum_arrived(2 * per + m).wait_recv()
        sum_arrived(per + m).wait_recv()
        out_ref[:, m * step_cols : (m + 1) * step_cols] = psum[3 * per + m] + sum_land[2 * per + m] + sum_land[per + m]

    core_copy(my_rep).wait_send()

    @pl.when(mid == 0)
    def _():
        for c in range(pieces):
            for k in range(5):
                if (k, c) != (4, pieces - 1):
                    edge_send(k, c).wait_send()
        for j in range(3):
            for d, c in row_sends(j == 2):
                rows_copy(j, 0, d, c).wait_send()

    @pl.when(mid == 1)
    def _():
        for c in range(pieces):
            for k in range(4):
                far_send(k, c).wait_send()
            for j in range(3):
                home_send(j, c).wait_send()
        for d, c in row_sends(True):
            rows_copy(0, 0, d, c).wait_send()

    for n in range(3 * per):
        sum_send(n, 0, neighbour).wait_send()

    for n, i in enumerate(early):
        @pl.when(me != owner[i])
        def _():
            forward(i, n).wait_send()


def fused(inputs, grads, in_signs, out_signs, in_rows, out_rows, inv_gram):
    count = inputs.shape[0] // SEQ
    block_p = SKETCH // HIDDEN
    examples = 4 * count
    share = inv_gram.shape[1] // HIDDEN
    chunks = inv_gram.shape[1] // STEP
    f32 = jnp.float32
    dma = pltpu.SemaphoreType.DMA
    vmem = pl.BlockSpec(memory_space=pltpu.VMEM)
    hbm = pl.BlockSpec(memory_space=pl.ANY)
    return pl.pallas_call(
        fused_kernel,
        out_shape=pltpu.VMEM((examples, share), f32),
        in_specs=[hbm] * 7,
        out_specs=vmem,
        scratch_shapes=[
            pltpu.VMEM((inputs.shape[1] // LANES, LANES), jnp.int32),
            pltpu.VMEM((grads.shape[1] // LANES, LANES), jnp.int32),
            pltpu.VMEM((1, SKETCH), jnp.int32),
            pltpu.VMEM((1, SKETCH), jnp.int32),
            dma((4,)),
            pltpu.VMEM((count, SEQ, inputs.shape[1]), jnp.bfloat16),
            pltpu.VMEM((count, SEQ, grads.shape[1]), jnp.bfloat16),
            pltpu.VMEM(inv_gram.shape, jnp.bfloat16),
            pltpu.VMEM((inputs.shape[1], SKETCH), jnp.bfloat16),
            pltpu.VMEM((grads.shape[1], SKETCH), jnp.bfloat16),
            pltpu.VMEM((count, 2, SEQ, SKETCH), f32),
            pltpu.VMEM((5, 2, SEQ, SKETCH), f32),
            pltpu.VMEM((4, 2, SEQ, SKETCH), f32),
            pltpu.VMEM((3, SKETCH, SKETCH), f32),
            pltpu.VMEM((examples, block_p, SKETCH), f32),
            pltpu.VMEM((2 * examples, block_p * SKETCH), jnp.bfloat16),
            pltpu.VMEM((chunks, examples, STEP), f32),
            pltpu.VMEM((3 * chunks // HIDDEN, examples, STEP), f32),
            dma((count,)),
            dma((count,)),
            dma((4,)),
            dma((count, PIECES)),
            dma((5, PIECES)),
            dma((4, PIECES)),
            dma((3, HIDDEN, 2)),
            dma((4,)),
            dma((2, count)),
            dma,
            dma,
            dma((chunks,)),
            dma((3 * chunks // HIDDEN,)),
        ],
        compiler_params=pltpu.CompilerParams(
            collective_id=0, has_side_effects=True, vmem_limit_bytes=63 << 20
        ),
    )(
        inputs,
        grads,
        in_signs.reshape(inputs.shape[1] // LANES, LANES),
        out_signs.reshape(grads.shape[1] // LANES, LANES),
        in_rows.reshape(1, SKETCH),
        out_rows.reshape(1, SKETCH),
        inv_gram,
    )


def plain_sketch(values, signs, rows, width, shard):
    inner = width // HAD
    local_high = values.shape[1] // inner
    high, low = rows // inner, rows % inner
    feature = jnp.arange(values.shape[1], dtype=jnp.int32)
    sources = shard * local_high + feature // inner
    sign = (1 - 2 * had_parity(high[None, :], sources[:, None])) * signs[:, None]
    hit = (feature % inner)[:, None] == low[None, :]
    matrix = jnp.where(hit, sign.astype(jnp.float32) / math.sqrt(HAD), 0.0)
    return jnp.dot(values, matrix.astype(jnp.bfloat16), preferred_element_type=jnp.float32)


def plain(inputs, grads, in_signs, out_signs, in_rows, out_rows, inv_gram):
    shard = lax.axis_index("hidden")
    out_part = plain_sketch(grads, out_signs, out_rows, OUT_W, shard)
    in_part = plain_sketch(inputs, in_signs, in_rows, IN_W, shard)
    block_p = inv_gram.shape[0] // SKETCH
    count = inputs.shape[0] // SEQ
    out_mine = lax.psum_scatter(out_part, "hidden", scatter_dimension=1, tiled=True)
    in_sketch = lax.psum(in_part, "hidden")
    projected = jnp.einsum(
        "esp,esq->epq",
        out_mine.reshape(count, SEQ, block_p),
        in_sketch.reshape(count, SEQ, SKETCH),
        precision=lax.Precision.HIGHEST,
    )
    projected = projected.reshape(count, block_p * SKETCH)
    partial_out = jnp.dot(
        lax.all_gather(projected, ("cols", "rep"), axis=0, tiled=True),
        inv_gram.astype(jnp.float32),
        precision=lax.Precision.HIGHEST,
        preferred_element_type=jnp.float32,
    )
    return lax.psum_scatter(partial_out, "hidden", scatter_dimension=1, tiled=True)


def solution(mesh):
    dims = tuple(mesh.shape[name] for name in ("hidden", "cols", "rep"))

    def on_device(inputs, *rest):
        if dims == (HIDDEN, 2, 2) and inputs.shape[0] == 8 * SEQ:
            return fused(inputs, *rest)
        return plain(inputs, *rest)

    return jax.shard_map(
        on_device,
        mesh=mesh,
        in_specs=(
            P(("groups", "cols", "rep"), "hidden"),
            P(("groups", "cols", "rep"), "hidden"),
            P("hidden"),
            P("hidden"),
            P(),
            P(),
            P("hidden", ("cols", "rep")),
        ),
        out_specs=P("groups", ("cols", "rep", "hidden")),
        check_vma=False,
    )
```

```python
import functools
import math

import jax
import jax.numpy as jnp
from jax import lax
from jax.experimental import pallas as pl
from jax.experimental.pallas import tpu as pltpu
from jax.sharding import PartitionSpec as P

IN_W = 28672
OUT_W = 8192
HAD = 64
SKETCH = 128
SEQ = 128
LANES = 128
HIDDEN = 4
STEP = 512
PIECES = 4
LAG = 5
MESH = pl.DeviceIdType.MESH


def had_parity(left, right):
    both = jnp.bitwise_and(left, right)
    for shift in (4, 2, 1):
        both = jnp.bitwise_xor(both, jnp.right_shift(both, shift))
    return jnp.bitwise_and(both, 1)


def split_rows(rows, inner):
    high = jnp.floor((rows.astype(jnp.float32) + 0.5) * (1.0 / inner)).astype(jnp.int32)
    return high, rows - high * inner


def build_matrix(rows_ref, sign_ref, out_ref, shard, width):
    inner = width // HAD
    local_high = out_ref.shape[0] // inner
    high, low = split_rows(rows_ref[...], inner)
    hit = lax.broadcasted_iota(jnp.int32, (inner, SKETCH), 0) == low
    onehot = jnp.where(hit, 1.0, 0.0)
    sign = sign_ref[...].astype(jnp.float32).astype(jnp.bfloat16)
    line = lax.broadcasted_iota(jnp.int32, (sign.shape[0], SKETCH), 0)
    lane = lax.broadcasted_iota(jnp.int32, (LANES, SKETCH), 0)
    picked = {}
    for h in range(local_high):
        first, offset = divmod(h * inner, LANES)
        at = offset + low
        if offset not in picked:
            pick = jnp.where(lane == jnp.bitwise_and(at, LANES - 1), 1.0, 0.0).astype(jnp.bfloat16)
            picked[offset] = jnp.dot(sign, pick, preferred_element_type=jnp.float32)
        own = line == first + jnp.right_shift(at, LANES.bit_length() - 1)
        coef = jnp.sum(jnp.where(own, picked[offset], 0.0), axis=0, keepdims=True)
        parity = had_parity(high, shard * local_high + h)
        coef = coef * (1 - 2 * parity).astype(jnp.float32) * (1.0 / math.sqrt(HAD))
        out_ref[h * inner : (h + 1) * inner, :] = (onehot * coef).astype(jnp.bfloat16)


def fused_kernel(
    x_ref,
    g_ref,
    in_sign_ref,
    out_sign_ref,
    in_rows_ref,
    out_rows_ref,
    gram_ref,
    out_ref,
    in_sign,
    out_sign,
    in_rows,
    out_rows,
    small_sem,
    x_buf,
    g_buf,
    gram_buf,
    mat_in,
    mat_out,
    part,
    land_edge,
    land_far,
    proj,
    allp,
    wide,
    psum,
    sum_land,
    x_sem,
    g_sem,
    gram_sem,
    send_part,
    recv_edge,
    recv_far,
    send_rows,
    send_fwd,
    recv_rows,
    send_core,
    recv_core,
    send_sum,
    recv_sum,
):
    me = lax.axis_index("hidden")
    my_col = lax.axis_index("cols")
    my_rep = lax.axis_index("rep")
    count = x_buf.shape[0]
    side = me // 2
    mid = lax.rem((me + 1) // 2, 2)
    own_edge, own_mid, far_mid = 3 * side, 1 + side, 2 - side
    block_p = SKETCH // HIDDEN
    chunks = psum.shape[0]
    step_cols = psum.shape[2]

    def example(k):
        early = 1 - (k + count - 3) // count
        label = count - 1 - k + early * (2 * k - 2)
        return label + side * (count - 1 - 2 * label)

    def load_x(k):
        row = pl.multiple_of(example(k) * SEQ, SEQ)
        return pltpu.make_async_copy(x_ref.at[pl.ds(row, SEQ)], x_buf.at[k], x_sem.at[k])

    def load_g(k):
        row = pl.multiple_of(example(k) * SEQ, SEQ)
        return pltpu.make_async_copy(g_ref.at[pl.ds(row, SEQ)], g_buf.at[k], g_sem.at[k])

    gram_parts = gram_sem.shape[0]
    gram_rows = gram_ref.shape[0] // gram_parts

    def load_gram(k):
        where = pl.ds(k * gram_rows, gram_rows)
        return pltpu.make_async_copy(gram_ref.at[where], gram_buf.at[where], gram_sem.at[k])

    small = [(out_rows_ref, out_rows), (out_sign_ref, out_sign), (in_rows_ref, in_rows), (in_sign_ref, in_sign)]
    loads = [pltpu.make_async_copy(far, near, small_sem.at[n]) for n, (far, near) in enumerate(small)]
    for load in loads:
        load.start()
    load_g(0).start()
    load_x(0).start()

    barrier = pltpu.get_barrier_semaphore()
    pl.semaphore_signal(barrier, inc=1, device_id={"rep": 1 - my_rep}, device_id_type=MESH)
    pl.semaphore_signal(barrier, inc=1, device_id={"cols": 1 - my_col}, device_id_type=MESH)
    pl.semaphore_signal(barrier, inc=1, device_id={"hidden": own_edge + own_mid - me}, device_id_type=MESH)

    @pl.when(mid == 1)
    def _():
        pl.semaphore_signal(barrier, inc=1, device_id={"hidden": far_mid}, device_id_type=MESH)

    for load in loads:
        load.wait()
    for k in range(1, count):
        load_g(k).start()
        load_x(k).start()
    build_matrix(out_rows, out_sign, mat_out, me, OUT_W)
    build_matrix(in_rows, in_sign, mat_in, me, IN_W)

    pieces = send_part.shape[1]
    piece = 2 * SEQ // pieces

    def cut(ref, k, c):
        row = pl.multiple_of(lax.rem(c, pieces // 2) * piece, piece)
        return ref.at[k, c // (pieces // 2), pl.ds(row, piece)]

    def edge_send(k, c):
        return pltpu.make_async_remote_copy(
            src_ref=cut(part, k, c),
            dst_ref=cut(land_edge, k, c),
            send_sem=send_part.at[k, c],
            recv_sem=recv_edge.at[k, c],
            device_id={"hidden": own_mid},
            device_id_type=MESH,
        )

    def far_send(k, c):
        return pltpu.make_async_remote_copy(
            src_ref=cut(part, k, c),
            dst_ref=cut(land_far, k, c),
            send_sem=send_part.at[k, c],
            recv_sem=recv_far.at[k, c],
            device_id={"hidden": far_mid},
            device_id_type=MESH,
        )

    def home_send(j, c):
        return pltpu.make_async_remote_copy(
            src_ref=cut(part, 5 + j, c),
            dst_ref=cut(land_far, j, c),
            send_sem=send_part.at[5 + j, c],
            recv_sem=recv_far.at[j, c],
            device_id={"hidden": own_edge},
            device_id_type=MESH,
        )

    def edge_arrived(k, c):
        return pltpu.make_async_remote_copy(
            src_ref=cut(part, k, c),
            dst_ref=cut(land_edge, k, c),
            send_sem=send_part.at[k, c],
            recv_sem=recv_edge.at[k, c],
            device_id={"rep": 1 - my_rep},
            device_id_type=MESH,
        )

    def far_arrived(k, c):
        return pltpu.make_async_remote_copy(
            src_ref=cut(part, k, c),
            dst_ref=cut(land_far, k, c),
            send_sem=send_part.at[k, c],
            recv_sem=recv_far.at[k, c],
            device_id={"rep": 1 - my_rep},
            device_id_type=MESH,
        )

    def add(k, c, landed):
        here = cut(part, k, c)
        here[...] = here[...] + landed[...]

    def relay_edge(n):
        k, c = n // pieces, lax.rem(n, pieces)
        edge_arrived(k, c).wait_recv()
        add(k, c, cut(land_edge, k, c))
        far_send(k, c).start()

    def relay_home(n):
        j, c = n // pieces, lax.rem(n, pieces)
        far_arrived(j, c).wait_recv()
        add(5 + j, c, cut(land_far, j, c))
        home_send(j, c).start()

    def turn(n):
        relay_edge(n)

        @pl.when(n >= LAG)
        def _():
            relay_home(n - LAG)

    def sketch_step(k, carry):
        sends = jnp.logical_and(mid == 0, k < 5)
        load_g(k).wait()
        part[k, 0] = jnp.dot(g_buf[k], mat_out[...], preferred_element_type=jnp.float32)

        @pl.when(k == 3 * mid)
        def _():
            pl.semaphore_wait(barrier, 3 + mid)

        @pl.when(sends)
        def _():
            for c in range(pieces // 2):
                edge_send(k, c).start()

        load_x(k).wait()
        part[k, 1] = jnp.dot(x_buf[k], mat_in[...], preferred_element_type=jnp.float32)

        @pl.when(sends)
        def _():
            for c in range(pieces // 2, pieces):
                edge_send(k, c).start()

        @pl.when(jnp.logical_and(mid == 1, k >= 3))
        def _():
            for n in range(2):
                turn(2 * (k - 3) + n)

        return carry

    lax.fori_loop(0, count, sketch_step, 0)
    for k in range(gram_parts):
        load_gram(k).start()

    def split(value):
        upper = value.astype(jnp.bfloat16)
        return upper, (value - upper.astype(jnp.float32)).astype(jnp.bfloat16)

    def project(k, slot):
        left, left_low = split(part[k, 0])
        right, right_low = split(part[k, 1])
        proj[slot] = lax.dot_general(
            jnp.concatenate([left, left, left_low]),
            jnp.concatenate([right, right_low, right]),
            (((0,), (0,)), ((), ())),
            preferred_element_type=jnp.float32,
        )

    def place(rep, col, i):
        return (rep * 2 + col) * count + i

    def rows_copy(slot, i, d, c):
        z = (me, 3 - 3 * side, far_mid, own_edge + own_mid - me)[d]
        col = my_col + c * (1 - 2 * my_col)
        return pltpu.make_async_remote_copy(
            src_ref=proj.at[slot, pl.ds(pl.multiple_of(z * block_p, block_p), block_p), :],
            dst_ref=allp.at[place(my_rep, my_col, i)],
            send_sem=send_rows.at[slot, d, c],
            recv_sem=recv_rows.at[my_col, i],
            device_id={"hidden": z, "cols": col},
            device_id_type=MESH,
        )

    def forward(i, n):
        block = allp.at[place(my_rep, my_col, i)]
        return pltpu.make_async_remote_copy(
            src_ref=block,
            dst_ref=block,
            send_sem=send_fwd.at[n],
            recv_sem=recv_rows.at[my_col, i],
            device_id={"cols": 1 - my_col},
            device_id_type=MESH,
        )

    def rows_arrived(col, i):
        block = allp.at[place(my_rep, col, i)]
        return pltpu.make_async_remote_copy(
            src_ref=block,
            dst_ref=block,
            send_sem=send_fwd.at[0],
            recv_sem=recv_rows.at[col, i],
            device_id={"cols": 1 - my_col},
            device_id_type=MESH,
        )

    def row_sends(late):
        both = [(d, c) for d in (1, 2, 3, 0) for c in (1, 0) if (d, c) != (0, 0)]
        return both if late else [(d, c) for d, c in both if d == 0 or c == 0]

    def distribute(slot, i, late):
        for d, c in row_sends(late):
            rows_copy(slot, i, d, c).start()
        allp[place(my_rep, my_col, i)] = proj[slot, pl.ds(pl.multiple_of(me * block_p, block_p), block_p), :]

    @pl.when(mid == 1)
    def _():
        def later(n, carry):
            turn(n)
            return carry

        lax.fori_loop(2 * (count - 3), 4 * pieces, later, 0)

        def rest(n, carry):
            relay_home(n)
            return carry

        lax.fori_loop(4 * pieces - LAG, 3 * pieces, rest, 0)
        for c in range(pieces):
            edge_arrived(4, c).wait_recv()
            far_arrived(3, c).wait_recv()
            add(4, c, cut(land_edge, 4, c))
            add(4, c, cut(land_far, 3, c))
        project(4, 0)
        distribute(0, 3 + side, True)

    @pl.when(mid == 0)
    def _():
        for j in range(3):
            for c in range(pieces):
                far_arrived(j, c).wait_recv()
                add(5 + j, c, cut(land_far, j, c))
            project(5 + j, j)
            if j == 0:
                edge_send(4, pieces - 1).wait_send()
            distribute(j, example(5 + j), j == 2)

    owner = [0, 0, 0, 1, 2, 3, 3, 3]
    early = (1, 2, 5, 6)
    for n, i in enumerate(early):
        @pl.when(me != owner[i])
        def _():
            rows_arrived(my_col, i).wait_recv()
            forward(i, n).start()

    for i in range(count):
        if i not in early:
            @pl.when(me != owner[i])
            def _():
                rows_arrived(my_col, i).wait_recv()

    for i in range(count):
        rows_arrived(1 - my_col, i).wait_recv()

    def core_copy(rep):
        block = allp.at[pl.ds(rep * 2 * count, 2 * count)]
        return pltpu.make_async_remote_copy(
            src_ref=block,
            dst_ref=block,
            send_sem=send_core,
            recv_sem=recv_core,
            device_id={"rep": 1 - my_rep},
            device_id_type=MESH,
        )

    def widen(rep):
        first = pl.multiple_of(rep * 2 * count, 2 * count)
        for p in range(block_p):
            rows = allp[pl.ds(first, 2 * count), p, :]
            upper = rows.astype(jnp.bfloat16)
            wide[pl.ds(first, 2 * count), p * SKETCH : (p + 1) * SKETCH] = upper
            lower = (rows - upper.astype(jnp.float32)).astype(jnp.bfloat16)
            wide[pl.ds(4 * count + first, 2 * count), p * SKETCH : (p + 1) * SKETCH] = lower

    core_copy(my_rep).start()
    widen(my_rep)
    core_copy(1 - my_rep).wait_recv()
    widen(1 - my_rep)
    for k in range(gram_parts):
        load_gram(k).wait()

    examples = 4 * count
    per = chunks // HIDDEN

    def sum_send(n, m, z):
        return pltpu.make_async_remote_copy(
            src_ref=psum.at[n],
            dst_ref=sum_land.at[m],
            send_sem=send_sum.at[n],
            recv_sem=recv_sum.at[m],
            device_id={"hidden": z},
            device_id_type=MESH,
        )

    def sum_arrived(m):
        return pltpu.make_async_remote_copy(
            src_ref=psum.at[0],
            dst_ref=sum_land.at[m],
            send_sem=send_sum.at[0],
            recv_sem=recv_sum.at[m],
            device_id={"rep": 1 - my_rep},
            device_id_type=MESH,
        )

    def kind(d, value):
        return 1 - (lax.rem(d + HIDDEN - value, HIDDEN) + HIDDEN - 1) // HIDDEN

    far_edge, neighbour = 3 - 3 * side, own_edge + own_mid - me

    def gram_step(n, carry):
        d = n // per
        place_d = kind(d, mid * 2) * far_mid + kind(d, 1 - mid) * far_edge + kind(d, 2 - mid) * neighbour + kind(d, 3) * me
        column = pl.multiple_of((place_d * per + lax.rem(n, per)) * step_cols, step_cols)
        both = jnp.dot(wide[...], gram_buf[:, pl.ds(column, step_cols)], preferred_element_type=jnp.float32)
        total = both[:examples] + both[examples:]
        for rep in range(2):
            for col in range(2):
                a, b = (rep * 2 + col) * count, (col * 2 + rep) * count
                psum[n, b : b + count, :] = total[a : a + count]

        m = lax.rem(n, per)

        @pl.when(jnp.logical_and(mid == 0, d == 0))
        def _():
            sum_send(n, m, own_mid).start()

        @pl.when(d == 1 - mid)
        def _():
            sum_send(n, (2 - mid) * per + m, far_edge).start()

        @pl.when(d == 2 - mid)
        def _():
            sum_send(n, (1 - mid) * per + m, neighbour).start()

        @pl.when(jnp.logical_and(mid == 1, d == 2))
        def _():
            sum_arrived(m).wait_recv()
            psum[n] = psum[n] + sum_land[m]
            sum_send(n, 2 * per + m, far_mid).start()

        return carry

    lax.fori_loop(0, chunks, gram_step, 0)

    for m in range(per):
        @pl.when(mid == 0)
        def _():
            sum_arrived(m).wait_recv()
            psum[3 * per + m] = psum[3 * per + m] + sum_land[m]

        sum_arrived(2 * per + m).wait_recv()
        sum_arrived(per + m).wait_recv()
        out_ref[:, m * step_cols : (m + 1) * step_cols] = psum[3 * per + m] + sum_land[2 * per + m] + sum_land[per + m]

    core_copy(my_rep).wait_send()

    @pl.when(mid == 0)
    def _():
        for c in range(pieces):
            for k in range(5):
                if (k, c) != (4, pieces - 1):
                    edge_send(k, c).wait_send()
        for j in range(3):
            for d, c in row_sends(j == 2):
                rows_copy(j, 0, d, c).wait_send()

    @pl.when(mid == 1)
    def _():
        for c in range(pieces):
            for k in range(4):
                far_send(k, c).wait_send()
            for j in range(3):
                home_send(j, c).wait_send()
        for d, c in row_sends(True):
            rows_copy(0, 0, d, c).wait_send()

    for n in range(3 * per):
        sum_send(n, 0, neighbour).wait_send()

    for n, i in enumerate(early):
        @pl.when(me != owner[i])
        def _():
            forward(i, n).wait_send()


def fused(inputs, grads, in_signs, out_signs, in_rows, out_rows, inv_gram):
    count = inputs.shape[0] // SEQ
    block_p = SKETCH // HIDDEN
    examples = 4 * count
    share = inv_gram.shape[1] // HIDDEN
    chunks = inv_gram.shape[1] // STEP
    f32 = jnp.float32
    dma = pltpu.SemaphoreType.DMA
    vmem = pl.BlockSpec(memory_space=pltpu.VMEM)
    hbm = pl.BlockSpec(memory_space=pl.ANY)
    return pl.pallas_call(
        fused_kernel,
        out_shape=pltpu.VMEM((examples, share), f32),
        in_specs=[hbm] * 7,
        out_specs=vmem,
        scratch_shapes=[
            pltpu.VMEM((inputs.shape[1] // LANES, LANES), jnp.int32),
            pltpu.VMEM((grads.shape[1] // LANES, LANES), jnp.int32),
            pltpu.VMEM((1, SKETCH), jnp.int32),
            pltpu.VMEM((1, SKETCH), jnp.int32),
            dma((4,)),
            pltpu.VMEM((count, SEQ, inputs.shape[1]), jnp.bfloat16),
            pltpu.VMEM((count, SEQ, grads.shape[1]), jnp.bfloat16),
            pltpu.VMEM(inv_gram.shape, jnp.bfloat16),
            pltpu.VMEM((inputs.shape[1], SKETCH), jnp.bfloat16),
            pltpu.VMEM((grads.shape[1], SKETCH), jnp.bfloat16),
            pltpu.VMEM((count, 2, SEQ, SKETCH), f32),
            pltpu.VMEM((5, 2, SEQ, SKETCH), f32),
            pltpu.VMEM((4, 2, SEQ, SKETCH), f32),
            pltpu.VMEM((3, SKETCH, SKETCH), f32),
            pltpu.VMEM((examples, block_p, SKETCH), f32),
            pltpu.VMEM((2 * examples, block_p * SKETCH), jnp.bfloat16),
            pltpu.VMEM((chunks, examples, STEP), f32),
            pltpu.VMEM((3 * chunks // HIDDEN, examples, STEP), f32),
            dma((count,)),
            dma((count,)),
            dma((4,)),
            dma((count, PIECES)),
            dma((5, PIECES)),
            dma((4, PIECES)),
            dma((3, HIDDEN, 2)),
            dma((4,)),
            dma((2, count)),
            dma,
            dma,
            dma((chunks,)),
            dma((3 * chunks // HIDDEN,)),
        ],
        compiler_params=pltpu.CompilerParams(
            collective_id=0, has_side_effects=True, vmem_limit_bytes=63 << 20
        ),
    )(
        inputs,
        grads,
        in_signs.reshape(inputs.shape[1] // LANES, LANES),
        out_signs.reshape(grads.shape[1] // LANES, LANES),
        in_rows.reshape(1, SKETCH),
        out_rows.reshape(1, SKETCH),
        inv_gram,
    )


def plain_sketch(values, signs, rows, width, shard):
    inner = width // HAD
    local_high = values.shape[1] // inner
    high, low = rows // inner, rows % inner
    feature = jnp.arange(values.shape[1], dtype=jnp.int32)
    sources = shard * local_high + feature // inner
    sign = (1 - 2 * had_parity(high[None, :], sources[:, None])) * signs[:, None]
    hit = (feature % inner)[:, None] == low[None, :]
    matrix = jnp.where(hit, sign.astype(jnp.float32) / math.sqrt(HAD), 0.0)
    return jnp.dot(values, matrix.astype(jnp.bfloat16), preferred_element_type=jnp.float32)


def plain(inputs, grads, in_signs, out_signs, in_rows, out_rows, inv_gram):
    shard = lax.axis_index("hidden")
    out_part = plain_sketch(grads, out_signs, out_rows, OUT_W, shard)
    in_part = plain_sketch(inputs, in_signs, in_rows, IN_W, shard)
    block_p = inv_gram.shape[0] // SKETCH
    count = inputs.shape[0] // SEQ
    out_mine = lax.psum_scatter(out_part, "hidden", scatter_dimension=1, tiled=True)
    in_sketch = lax.psum(in_part, "hidden")
    projected = jnp.einsum(
        "esp,esq->epq",
        out_mine.reshape(count, SEQ, block_p),
        in_sketch.reshape(count, SEQ, SKETCH),
        precision=lax.Precision.HIGHEST,
    )
    projected = projected.reshape(count, block_p * SKETCH)
    partial_out = jnp.dot(
        lax.all_gather(projected, ("cols", "rep"), axis=0, tiled=True),
        inv_gram.astype(jnp.float32),
        precision=lax.Precision.HIGHEST,
        preferred_element_type=jnp.float32,
    )
    return lax.psum_scatter(partial_out, "hidden", scatter_dimension=1, tiled=True)


def solution(mesh):
    dims = tuple(mesh.shape[name] for name in ("hidden", "cols", "rep"))

    def on_device(inputs, *rest):
        if dims == (HIDDEN, 2, 2) and inputs.shape[0] == 8 * SEQ:
            return fused(inputs, *rest)
        return plain(inputs, *rest)

    return jax.shard_map(
        on_device,
        mesh=mesh,
        in_specs=(
            P(("groups", "cols", "rep"), "hidden"),
            P(("groups", "cols", "rep"), "hidden"),
            P("hidden"),
            P("hidden"),
            P(),
            P(),
            P("hidden", ("cols", "rep")),
        ),
        out_specs=P("groups", ("cols", "rep", "hidden")),
        check_vma=False,
    )
```

```python
import functools
import math

import jax
import jax.numpy as jnp
from jax import lax
from jax.experimental import pallas as pl
from jax.experimental.pallas import tpu as pltpu
from jax.sharding import PartitionSpec as P

IN_W = 28672
OUT_W = 8192
HAD = 64
SKETCH = 128
SEQ = 128
LANES = 128
HIDDEN = 4
STEP = 512
PIECES = 4
LAG = 5
MESH = pl.DeviceIdType.MESH


def had_parity(left, right):
    both = jnp.bitwise_and(left, right)
    for shift in (4, 2, 1):
        both = jnp.bitwise_xor(both, jnp.right_shift(both, shift))
    return jnp.bitwise_and(both, 1)


def split_rows(rows, inner):
    high = jnp.floor((rows.astype(jnp.float32) + 0.5) * (1.0 / inner)).astype(jnp.int32)
    return high, rows - high * inner


def build_matrix(rows_ref, sign_ref, out_ref, shard, width):
    inner = width // HAD
    local_high = out_ref.shape[0] // inner
    high, low = split_rows(rows_ref[...], inner)
    hit = lax.broadcasted_iota(jnp.int32, (inner, SKETCH), 0) == low
    onehot = jnp.where(hit, 1.0, 0.0)
    sign = sign_ref[...].astype(jnp.float32).astype(jnp.bfloat16)
    line = lax.broadcasted_iota(jnp.int32, (sign.shape[0], SKETCH), 0)
    lane = lax.broadcasted_iota(jnp.int32, (LANES, SKETCH), 0)
    picked = {}
    for h in range(local_high):
        first, offset = divmod(h * inner, LANES)
        at = offset + low
        if offset not in picked:
            pick = jnp.where(lane == jnp.bitwise_and(at, LANES - 1), 1.0, 0.0).astype(jnp.bfloat16)
            picked[offset] = jnp.dot(sign, pick, preferred_element_type=jnp.float32)
        own = line == first + jnp.right_shift(at, LANES.bit_length() - 1)
        coef = jnp.sum(jnp.where(own, picked[offset], 0.0), axis=0, keepdims=True)
        parity = had_parity(high, shard * local_high + h)
        coef = coef * (1 - 2 * parity).astype(jnp.float32) * (1.0 / math.sqrt(HAD))
        out_ref[h * inner : (h + 1) * inner, :] = (onehot * coef).astype(jnp.bfloat16)


def fused_kernel(
    x_ref,
    g_ref,
    in_sign_ref,
    out_sign_ref,
    in_rows_ref,
    out_rows_ref,
    gram_ref,
    out_ref,
    in_sign,
    out_sign,
    in_rows,
    out_rows,
    small_sem,
    x_buf,
    g_buf,
    gram_buf,
    mat_in,
    mat_out,
    part,
    land_edge,
    land_far,
    proj,
    allp,
    wide,
    psum,
    sum_land,
    x_sem,
    g_sem,
    gram_sem,
    send_part,
    recv_edge,
    recv_far,
    send_rows,
    send_fwd,
    recv_rows,
    send_core,
    recv_core,
    send_sum,
    recv_sum,
):
    me = lax.axis_index("hidden")
    my_col = lax.axis_index("cols")
    my_rep = lax.axis_index("rep")
    count = x_buf.shape[0]
    side = me // 2
    mid = lax.rem((me + 1) // 2, 2)
    own_edge, own_mid, far_mid = 3 * side, 1 + side, 2 - side
    block_p = SKETCH // HIDDEN
    chunks = psum.shape[0]
    step_cols = psum.shape[2]

    def example(k):
        early = 1 - (k + count - 3) // count
        label = count - 1 - k + early * (2 * k - 2)
        return label + side * (count - 1 - 2 * label)

    def load_x(k):
        row = pl.multiple_of(example(k) * SEQ, SEQ)
        return pltpu.make_async_copy(x_ref.at[pl.ds(row, SEQ)], x_buf.at[k], x_sem.at[k])

    def load_g(k):
        row = pl.multiple_of(example(k) * SEQ, SEQ)
        return pltpu.make_async_copy(g_ref.at[pl.ds(row, SEQ)], g_buf.at[k], g_sem.at[k])

    gram_parts = gram_sem.shape[0]
    gram_rows = gram_ref.shape[0] // gram_parts

    def load_gram(k):
        where = pl.ds(k * gram_rows, gram_rows)
        return pltpu.make_async_copy(gram_ref.at[where], gram_buf.at[where], gram_sem.at[k])

    small = [(out_rows_ref, out_rows), (out_sign_ref, out_sign), (in_rows_ref, in_rows), (in_sign_ref, in_sign)]
    loads = [pltpu.make_async_copy(far, near, small_sem.at[n]) for n, (far, near) in enumerate(small)]
    for load in loads:
        load.start()
    load_g(0).start()
    load_x(0).start()

    barrier = pltpu.get_barrier_semaphore()
    pl.semaphore_signal(barrier, inc=1, device_id={"rep": 1 - my_rep}, device_id_type=MESH)
    pl.semaphore_signal(barrier, inc=1, device_id={"cols": 1 - my_col}, device_id_type=MESH)
    pl.semaphore_signal(barrier, inc=1, device_id={"hidden": own_edge + own_mid - me}, device_id_type=MESH)

    @pl.when(mid == 1)
    def _():
        pl.semaphore_signal(barrier, inc=1, device_id={"hidden": far_mid}, device_id_type=MESH)

    for load in loads:
        load.wait()
    for k in range(1, count):
        load_g(k).start()
        load_x(k).start()
    build_matrix(out_rows, out_sign, mat_out, me, OUT_W)
    build_matrix(in_rows, in_sign, mat_in, me, IN_W)

    pieces = send_part.shape[1]
    piece = 2 * SEQ // pieces

    def cut(ref, k, c):
        row = pl.multiple_of(lax.rem(c, pieces // 2) * piece, piece)
        return ref.at[k, c // (pieces // 2), pl.ds(row, piece)]

    def edge_send(k, c):
        return pltpu.make_async_remote_copy(
            src_ref=cut(part, k, c),
            dst_ref=cut(land_edge, k, c),
            send_sem=send_part.at[k, c],
            recv_sem=recv_edge.at[k, c],
            device_id={"hidden": own_mid},
            device_id_type=MESH,
        )

    def far_send(k, c):
        return pltpu.make_async_remote_copy(
            src_ref=cut(part, k, c),
            dst_ref=cut(land_far, k, c),
            send_sem=send_part.at[k, c],
            recv_sem=recv_far.at[k, c],
            device_id={"hidden": far_mid},
            device_id_type=MESH,
        )

    def home_send(j, c):
        return pltpu.make_async_remote_copy(
            src_ref=cut(part, 5 + j, c),
            dst_ref=cut(land_far, j, c),
            send_sem=send_part.at[5 + j, c],
            recv_sem=recv_far.at[j, c],
            device_id={"hidden": own_edge},
            device_id_type=MESH,
        )

    def edge_arrived(k, c):
        return pltpu.make_async_remote_copy(
            src_ref=cut(part, k, c),
            dst_ref=cut(land_edge, k, c),
            send_sem=send_part.at[k, c],
            recv_sem=recv_edge.at[k, c],
            device_id={"rep": 1 - my_rep},
            device_id_type=MESH,
        )

    def far_arrived(k, c):
        return pltpu.make_async_remote_copy(
            src_ref=cut(part, k, c),
            dst_ref=cut(land_far, k, c),
            send_sem=send_part.at[k, c],
            recv_sem=recv_far.at[k, c],
            device_id={"rep": 1 - my_rep},
            device_id_type=MESH,
        )

    def add(k, c, landed):
        here = cut(part, k, c)
        here[...] = here[...] + landed[...]

    def relay_edge(n):
        k, c = n // pieces, lax.rem(n, pieces)
        edge_arrived(k, c).wait_recv()
        add(k, c, cut(land_edge, k, c))
        far_send(k, c).start()

    def relay_home(n):
        j, c = n // pieces, lax.rem(n, pieces)
        far_arrived(j, c).wait_recv()
        add(5 + j, c, cut(land_far, j, c))
        home_send(j, c).start()

    def turn(n):
        relay_edge(n)

        @pl.when(n >= LAG)
        def _():
            relay_home(n - LAG)

    def sketch_step(k, carry):
        sends = jnp.logical_and(mid == 0, k < 5)
        load_g(k).wait()
        part[k, 0] = jnp.dot(g_buf[k], mat_out[...], preferred_element_type=jnp.float32)

        @pl.when(k == 3 * mid)
        def _():
            pl.semaphore_wait(barrier, 3 + mid)

        @pl.when(sends)
        def _():
            for c in range(pieces // 2):
                edge_send(k, c).start()

        load_x(k).wait()
        part[k, 1] = jnp.dot(x_buf[k], mat_in[...], preferred_element_type=jnp.float32)

        @pl.when(sends)
        def _():
            for c in range(pieces // 2, pieces):
                edge_send(k, c).start()

        @pl.when(jnp.logical_and(mid == 1, k >= 3))
        def _():
            for n in range(2):
                turn(2 * (k - 3) + n)

        return carry

    lax.fori_loop(0, count, sketch_step, 0)
    for k in range(gram_parts):
        load_gram(k).start()

    def split(value):
        upper = value.astype(jnp.bfloat16)
        return upper, (value - upper.astype(jnp.float32)).astype(jnp.bfloat16)

    def project(k, slot):
        left, left_low = split(part[k, 0])
        right, right_low = split(part[k, 1])
        proj[slot] = lax.dot_general(
            jnp.concatenate([left, left, left_low]),
            jnp.concatenate([right, right_low, right]),
            (((0,), (0,)), ((), ())),
            preferred_element_type=jnp.float32,
        )

    def place(rep, col, i):
        return (rep * 2 + col) * count + i

    def rows_copy(slot, i, d, c):
        z = (me, 3 - 3 * side, far_mid, own_edge + own_mid - me)[d]
        col = my_col + c * (1 - 2 * my_col)
        return pltpu.make_async_remote_copy(
            src_ref=proj.at[slot, pl.ds(pl.multiple_of(z * block_p, block_p), block_p), :],
            dst_ref=allp.at[place(my_rep, my_col, i)],
            send_sem=send_rows.at[slot, d, c],
            recv_sem=recv_rows.at[my_col, i],
            device_id={"hidden": z, "cols": col},
            device_id_type=MESH,
        )

    def forward(i, n):
        block = allp.at[place(my_rep, my_col, i)]
        return pltpu.make_async_remote_copy(
            src_ref=block,
            dst_ref=block,
            send_sem=send_fwd.at[n],
            recv_sem=recv_rows.at[my_col, i],
            device_id={"cols": 1 - my_col},
            device_id_type=MESH,
        )

    def rows_arrived(col, i):
        block = allp.at[place(my_rep, col, i)]
        return pltpu.make_async_remote_copy(
            src_ref=block,
            dst_ref=block,
            send_sem=send_fwd.at[0],
            recv_sem=recv_rows.at[col, i],
            device_id={"cols": 1 - my_col},
            device_id_type=MESH,
        )

    def row_sends(late):
        both = [(d, c) for d in (1, 2, 3, 0) for c in (1, 0) if (d, c) != (0, 0)]
        return both if late else [(d, c) for d, c in both if d == 0 or c == 0]

    def keep(slot, i):
        allp[place(my_rep, my_col, i)] = proj[slot, pl.ds(pl.multiple_of(me * block_p, block_p), block_p), :]

    @pl.when(mid == 1)
    def _():
        def later(n, carry):
            turn(n)
            return carry

        lax.fori_loop(2 * (count - 3), 4 * pieces, later, 0)

        def rest(n, carry):
            relay_home(n)
            return carry

        lax.fori_loop(4 * pieces - LAG, 3 * pieces, rest, 0)
        for c in range(pieces):
            edge_arrived(4, c).wait_recv()
            far_arrived(3, c).wait_recv()
            add(4, c, cut(land_edge, 4, c))
            add(4, c, cut(land_far, 3, c))
        project(4, 0)
        for d, c in row_sends(True):
            rows_copy(0, 3 + side, d, c).start()
        keep(0, 3 + side)

    @pl.when(mid == 0)
    def _():
        def own(j, carry):
            for c in range(pieces):
                far_arrived(j, c).wait_recv()
                add(5 + j, c, cut(land_far, j, c))
            project(5 + j, j)
            i = example(5 + j)

            @pl.when(j == 0)
            def _():
                edge_send(4, pieces - 1).wait_send()

            @pl.when(j == 2)
            def _():
                for d in (1, 2, 3):
                    rows_copy(j, i, d, 1).start()

            for d in (1, 2, 3):
                rows_copy(j, i, d, 0).start()
            rows_copy(j, i, 0, 1).start()
            keep(j, i)
            return carry

        lax.fori_loop(0, 3, own, 0)

    owner = [0, 0, 0, 1, 2, 3, 3, 3]
    early = (1, 2, 5, 6)
    for n, i in enumerate(early):
        @pl.when(me != owner[i])
        def _():
            rows_arrived(my_col, i).wait_recv()
            forward(i, n).start()

    for i in range(count):
        if i not in early:
            @pl.when(me != owner[i])
            def _():
                rows_arrived(my_col, i).wait_recv()

    for i in range(count):
        rows_arrived(1 - my_col, i).wait_recv()

    def core_copy(rep):
        block = allp.at[pl.ds(rep * 2 * count, 2 * count)]
        return pltpu.make_async_remote_copy(
            src_ref=block,
            dst_ref=block,
            send_sem=send_core,
            recv_sem=recv_core,
            device_id={"rep": 1 - my_rep},
            device_id_type=MESH,
        )

    def widen(rep):
        first = pl.multiple_of(rep * 2 * count, 2 * count)
        for p in range(block_p):
            rows = allp[pl.ds(first, 2 * count), p, :]
            upper = rows.astype(jnp.bfloat16)
            wide[pl.ds(first, 2 * count), p * SKETCH : (p + 1) * SKETCH] = upper
            lower = (rows - upper.astype(jnp.float32)).astype(jnp.bfloat16)
            wide[pl.ds(4 * count + first, 2 * count), p * SKETCH : (p + 1) * SKETCH] = lower

    core_copy(my_rep).start()

    def widen_step(n, carry):
        @pl.when(n == 1)
        def _():
            core_copy(1 - my_rep).wait_recv()

        widen(my_rep + n * (1 - 2 * my_rep))
        return carry

    lax.fori_loop(0, 2, widen_step, 0)
    for k in range(gram_parts):
        load_gram(k).wait()

    examples = 4 * count
    per = chunks // HIDDEN

    def sum_send(n, m, z):
        return pltpu.make_async_remote_copy(
            src_ref=psum.at[n],
            dst_ref=sum_land.at[m],
            send_sem=send_sum.at[n],
            recv_sem=recv_sum.at[m],
            device_id={"hidden": z},
            device_id_type=MESH,
        )

    def sum_arrived(m):
        return pltpu.make_async_remote_copy(
            src_ref=psum.at[0],
            dst_ref=sum_land.at[m],
            send_sem=send_sum.at[0],
            recv_sem=recv_sum.at[m],
            device_id={"rep": 1 - my_rep},
            device_id_type=MESH,
        )

    def kind(d, value):
        return 1 - (lax.rem(d + HIDDEN - value, HIDDEN) + HIDDEN - 1) // HIDDEN

    far_edge, neighbour = 3 - 3 * side, own_edge + own_mid - me

    def gram_step(n, carry):
        d = n // per
        place_d = kind(d, mid * 2) * far_mid + kind(d, 1 - mid) * far_edge + kind(d, 2 - mid) * neighbour + kind(d, 3) * me
        column = pl.multiple_of((place_d * per + lax.rem(n, per)) * step_cols, step_cols)
        both = jnp.dot(wide[...], gram_buf[:, pl.ds(column, step_cols)], preferred_element_type=jnp.float32)
        total = both[:examples] + both[examples:]
        for rep in range(2):
            for col in range(2):
                a, b = (rep * 2 + col) * count, (col * 2 + rep) * count
                psum[n, b : b + count, :] = total[a : a + count]

        m = lax.rem(n, per)

        @pl.when(jnp.logical_and(mid == 0, d == 0))
        def _():
            sum_send(n, m, own_mid).start()

        @pl.when(d == 1 - mid)
        def _():
            sum_send(n, (2 - mid) * per + m, far_edge).start()

        @pl.when(d == 2 - mid)
        def _():
            sum_send(n, (1 - mid) * per + m, neighbour).start()

        @pl.when(jnp.logical_and(mid == 1, d == 2))
        def _():
            sum_arrived(m).wait_recv()
            psum[n] = psum[n] + sum_land[m]
            sum_send(n, 2 * per + m, far_mid).start()

        return carry

    lax.fori_loop(0, chunks, gram_step, 0)

    core_copy(my_rep).wait_send()

    @pl.when(mid == 0)
    def _():
        for c in range(pieces):
            for k in range(5):
                if (k, c) != (4, pieces - 1):
                    edge_send(k, c).wait_send()
        for j in range(3):
            for d, c in row_sends(j == 2):
                rows_copy(j, 0, d, c).wait_send()

    @pl.when(mid == 1)
    def _():
        for c in range(pieces):
            for k in range(4):
                far_send(k, c).wait_send()
            for j in range(3):
                home_send(j, c).wait_send()
        for d, c in row_sends(True):
            rows_copy(0, 0, d, c).wait_send()

    for n in range(3 * per):
        sum_send(n, 0, neighbour).wait_send()

    for n, i in enumerate(early):
        @pl.when(me != owner[i])
        def _():
            forward(i, n).wait_send()

    for m in range(per):
        @pl.when(mid == 0)
        def _():
            sum_arrived(m).wait_recv()
            psum[3 * per + m] = psum[3 * per + m] + sum_land[m]

        sum_arrived(2 * per + m).wait_recv()
        sum_arrived(per + m).wait_recv()
        out_ref[:, m * step_cols : (m + 1) * step_cols] = psum[3 * per + m] + sum_land[2 * per + m] + sum_land[per + m]


def fused(inputs, grads, in_signs, out_signs, in_rows, out_rows, inv_gram):
    count = inputs.shape[0] // SEQ
    block_p = SKETCH // HIDDEN
    examples = 4 * count
    share = inv_gram.shape[1] // HIDDEN
    chunks = inv_gram.shape[1] // STEP
    f32 = jnp.float32
    dma = pltpu.SemaphoreType.DMA
    vmem = pl.BlockSpec(memory_space=pltpu.VMEM)
    hbm = pl.BlockSpec(memory_space=pl.ANY)
    return pl.pallas_call(
        fused_kernel,
        out_shape=pltpu.VMEM((examples, share), f32),
        in_specs=[hbm] * 7,
        out_specs=vmem,
        scratch_shapes=[
            pltpu.VMEM((inputs.shape[1] // LANES, LANES), jnp.int32),
            pltpu.VMEM((grads.shape[1] // LANES, LANES), jnp.int32),
            pltpu.VMEM((1, SKETCH), jnp.int32),
            pltpu.VMEM((1, SKETCH), jnp.int32),
            dma((4,)),
            pltpu.VMEM((count, SEQ, inputs.shape[1]), jnp.bfloat16),
            pltpu.VMEM((count, SEQ, grads.shape[1]), jnp.bfloat16),
            pltpu.VMEM(inv_gram.shape, jnp.bfloat16),
            pltpu.VMEM((inputs.shape[1], SKETCH), jnp.bfloat16),
            pltpu.VMEM((grads.shape[1], SKETCH), jnp.bfloat16),
            pltpu.VMEM((count, 2, SEQ, SKETCH), f32),
            pltpu.VMEM((5, 2, SEQ, SKETCH), f32),
            pltpu.VMEM((4, 2, SEQ, SKETCH), f32),
            pltpu.VMEM((3, SKETCH, SKETCH), f32),
            pltpu.VMEM((examples, block_p, SKETCH), f32),
            pltpu.VMEM((2 * examples, block_p * SKETCH), jnp.bfloat16),
            pltpu.VMEM((chunks, examples, STEP), f32),
            pltpu.VMEM((3 * chunks // HIDDEN, examples, STEP), f32),
            dma((count,)),
            dma((count,)),
            dma((4,)),
            dma((count, PIECES)),
            dma((5, PIECES)),
            dma((4, PIECES)),
            dma((3, HIDDEN, 2)),
            dma((4,)),
            dma((2, count)),
            dma,
            dma,
            dma((chunks,)),
            dma((3 * chunks // HIDDEN,)),
        ],
        compiler_params=pltpu.CompilerParams(
            collective_id=0, has_side_effects=True, vmem_limit_bytes=63 << 20
        ),
    )(
        inputs,
        grads,
        in_signs.reshape(inputs.shape[1] // LANES, LANES),
        out_signs.reshape(grads.shape[1] // LANES, LANES),
        in_rows.reshape(1, SKETCH),
        out_rows.reshape(1, SKETCH),
        inv_gram,
    )


def plain_sketch(values, signs, rows, width, shard):
    inner = width // HAD
    local_high = values.shape[1] // inner
    high, low = rows // inner, rows % inner
    feature = jnp.arange(values.shape[1], dtype=jnp.int32)
    sources = shard * local_high + feature // inner
    sign = (1 - 2 * had_parity(high[None, :], sources[:, None])) * signs[:, None]
    hit = (feature % inner)[:, None] == low[None, :]
    matrix = jnp.where(hit, sign.astype(jnp.float32) / math.sqrt(HAD), 0.0)
    return jnp.dot(values, matrix.astype(jnp.bfloat16), preferred_element_type=jnp.float32)


def plain(inputs, grads, in_signs, out_signs, in_rows, out_rows, inv_gram):
    shard = lax.axis_index("hidden")
    out_part = plain_sketch(grads, out_signs, out_rows, OUT_W, shard)
    in_part = plain_sketch(inputs, in_signs, in_rows, IN_W, shard)
    block_p = inv_gram.shape[0] // SKETCH
    count = inputs.shape[0] // SEQ
    out_mine = lax.psum_scatter(out_part, "hidden", scatter_dimension=1, tiled=True)
    in_sketch = lax.psum(in_part, "hidden")
    projected = jnp.einsum(
        "esp,esq->epq",
        out_mine.reshape(count, SEQ, block_p),
        in_sketch.reshape(count, SEQ, SKETCH),
        precision=lax.Precision.HIGHEST,
    )
    projected = projected.reshape(count, block_p * SKETCH)
    partial_out = jnp.dot(
        lax.all_gather(projected, ("cols", "rep"), axis=0, tiled=True),
        inv_gram.astype(jnp.float32),
        precision=lax.Precision.HIGHEST,
        preferred_element_type=jnp.float32,
    )
    return lax.psum_scatter(partial_out, "hidden", scatter_dimension=1, tiled=True)


def solution(mesh):
    dims = tuple(mesh.shape[name] for name in ("hidden", "cols", "rep"))

    def on_device(inputs, *rest):
        if dims == (HIDDEN, 2, 2) and inputs.shape[0] == 8 * SEQ:
            return fused(inputs, *rest)
        return plain(inputs, *rest)

    return jax.shard_map(
        on_device,
        mesh=mesh,
        in_specs=(
            P(("groups", "cols", "rep"), "hidden"),
            P(("groups", "cols", "rep"), "hidden"),
            P("hidden"),
            P("hidden"),
            P(),
            P(),
            P("hidden", ("cols", "rep")),
        ),
        out_specs=P("groups", ("cols", "rep", "hidden")),
        check_vma=False,
    )
```

```python
import functools
import math

import jax
import jax.numpy as jnp
from jax import lax
from jax.experimental import pallas as pl
from jax.experimental.pallas import tpu as pltpu
from jax.sharding import PartitionSpec as P

IN_W = 28672
OUT_W = 8192
HAD = 64
SKETCH = 128
SEQ = 128
LANES = 128
HIDDEN = 4
STEP = 256
PIECES = 4
LAG = 5
MESH = pl.DeviceIdType.MESH


def had_parity(left, right):
    both = jnp.bitwise_and(left, right)
    for shift in (4, 2, 1):
        both = jnp.bitwise_xor(both, jnp.right_shift(both, shift))
    return jnp.bitwise_and(both, 1)


def split_rows(rows, inner):
    high = jnp.floor((rows.astype(jnp.float32) + 0.5) * (1.0 / inner)).astype(jnp.int32)
    return high, rows - high * inner


def build_matrix(rows_ref, sign_ref, out_ref, shard, width):
    inner = width // HAD
    local_high = out_ref.shape[0] // inner
    high, low = split_rows(rows_ref[...], inner)
    hit = lax.broadcasted_iota(jnp.int32, (inner, SKETCH), 0) == low
    onehot = jnp.where(hit, 1.0, 0.0)
    sign = sign_ref[...].astype(jnp.float32).astype(jnp.bfloat16)
    line = lax.broadcasted_iota(jnp.int32, (sign.shape[0], SKETCH), 0)
    lane = lax.broadcasted_iota(jnp.int32, (LANES, SKETCH), 0)
    picked = {}
    for h in range(local_high):
        first, offset = divmod(h * inner, LANES)
        at = offset + low
        if offset not in picked:
            pick = jnp.where(lane == jnp.bitwise_and(at, LANES - 1), 1.0, 0.0).astype(jnp.bfloat16)
            picked[offset] = jnp.dot(sign, pick, preferred_element_type=jnp.float32)
        own = line == first + jnp.right_shift(at, LANES.bit_length() - 1)
        coef = jnp.sum(jnp.where(own, picked[offset], 0.0), axis=0, keepdims=True)
        parity = had_parity(high, shard * local_high + h)
        coef = coef * (1 - 2 * parity).astype(jnp.float32) * (1.0 / math.sqrt(HAD))
        out_ref[h * inner : (h + 1) * inner, :] = (onehot * coef).astype(jnp.bfloat16)


def fused_kernel(
    x_ref,
    g_ref,
    in_sign_ref,
    out_sign_ref,
    in_rows_ref,
    out_rows_ref,
    gram_ref,
    out_ref,
    in_sign,
    out_sign,
    in_rows,
    out_rows,
    small_sem,
    x_buf,
    g_buf,
    gram_buf,
    mat_in,
    mat_out,
    part,
    land_edge,
    land_far,
    proj,
    allp,
    wide,
    psum,
    sum_land,
    x_sem,
    g_sem,
    gram_sem,
    send_part,
    recv_edge,
    recv_far,
    send_rows,
    send_fwd,
    recv_rows,
    send_core,
    recv_core,
    send_sum,
    recv_sum,
):
    me = lax.axis_index("hidden")
    my_col = lax.axis_index("cols")
    my_rep = lax.axis_index("rep")
    count = x_buf.shape[0]
    side = me // 2
    mid = lax.rem((me + 1) // 2, 2)
    own_edge, own_mid, far_mid = 3 * side, 1 + side, 2 - side
    block_p = SKETCH // HIDDEN
    chunks = psum.shape[0]
    step_cols = psum.shape[2]

    def example(k):
        early = 1 - (k + count - 3) // count
        label = count - 1 - k + early * (2 * k - 2)
        return label + side * (count - 1 - 2 * label)

    def load_x(k):
        row = pl.multiple_of(example(k) * SEQ, SEQ)
        return pltpu.make_async_copy(x_ref.at[pl.ds(row, SEQ)], x_buf.at[k], x_sem.at[k])

    def load_g(k):
        row = pl.multiple_of(example(k) * SEQ, SEQ)
        return pltpu.make_async_copy(g_ref.at[pl.ds(row, SEQ)], g_buf.at[k], g_sem.at[k])

    gram_parts = gram_sem.shape[0]
    gram_rows = gram_ref.shape[0] // gram_parts

    def load_gram(k):
        where = pl.ds(k * gram_rows, gram_rows)
        return pltpu.make_async_copy(gram_ref.at[where], gram_buf.at[where], gram_sem.at[k])

    small = [(out_rows_ref, out_rows), (out_sign_ref, out_sign), (in_rows_ref, in_rows), (in_sign_ref, in_sign)]
    loads = [pltpu.make_async_copy(far, near, small_sem.at[n]) for n, (far, near) in enumerate(small)]
    for load in loads:
        load.start()
    load_g(0).start()
    load_x(0).start()

    barrier = pltpu.get_barrier_semaphore()
    pl.semaphore_signal(barrier, inc=1, device_id={"rep": 1 - my_rep}, device_id_type=MESH)
    pl.semaphore_signal(barrier, inc=1, device_id={"cols": 1 - my_col}, device_id_type=MESH)
    pl.semaphore_signal(barrier, inc=1, device_id={"hidden": own_edge + own_mid - me}, device_id_type=MESH)

    @pl.when(mid == 1)
    def _():
        pl.semaphore_signal(barrier, inc=1, device_id={"hidden": far_mid}, device_id_type=MESH)

    for load in loads:
        load.wait()
    for k in range(1, count):
        load_g(k).start()
        load_x(k).start()
    build_matrix(out_rows, out_sign, mat_out, me, OUT_W)
    build_matrix(in_rows, in_sign, mat_in, me, IN_W)

    pieces = send_part.shape[1]
    piece = 2 * SEQ // pieces

    def cut(ref, k, c):
        row = pl.multiple_of(lax.rem(c, pieces // 2) * piece, piece)
        return ref.at[k, c // (pieces // 2), pl.ds(row, piece)]

    def edge_send(k, c):
        return pltpu.make_async_remote_copy(
            src_ref=cut(part, k, c),
            dst_ref=cut(land_edge, k, c),
            send_sem=send_part.at[k, c],
            recv_sem=recv_edge.at[k, c],
            device_id={"hidden": own_mid},
            device_id_type=MESH,
        )

    def far_send(k, c):
        return pltpu.make_async_remote_copy(
            src_ref=cut(part, k, c),
            dst_ref=cut(land_far, k, c),
            send_sem=send_part.at[k, c],
            recv_sem=recv_far.at[k, c],
            device_id={"hidden": far_mid},
            device_id_type=MESH,
        )

    def home_send(j, c):
        return pltpu.make_async_remote_copy(
            src_ref=cut(part, 5 + j, c),
            dst_ref=cut(land_far, j, c),
            send_sem=send_part.at[5 + j, c],
            recv_sem=recv_far.at[j, c],
            device_id={"hidden": own_edge},
            device_id_type=MESH,
        )

    def edge_arrived(k, c):
        return pltpu.make_async_remote_copy(
            src_ref=cut(part, k, c),
            dst_ref=cut(land_edge, k, c),
            send_sem=send_part.at[k, c],
            recv_sem=recv_edge.at[k, c],
            device_id={"rep": 1 - my_rep},
            device_id_type=MESH,
        )

    def far_arrived(k, c):
        return pltpu.make_async_remote_copy(
            src_ref=cut(part, k, c),
            dst_ref=cut(land_far, k, c),
            send_sem=send_part.at[k, c],
            recv_sem=recv_far.at[k, c],
            device_id={"rep": 1 - my_rep},
            device_id_type=MESH,
        )

    def add(k, c, landed):
        here = cut(part, k, c)
        here[...] = here[...] + landed[...]

    def relay_edge(n):
        k, c = n // pieces, lax.rem(n, pieces)
        edge_arrived(k, c).wait_recv()
        add(k, c, cut(land_edge, k, c))
        far_send(k, c).start()

    def relay_home(n):
        j, c = n // pieces, lax.rem(n, pieces)
        far_arrived(j, c).wait_recv()
        add(5 + j, c, cut(land_far, j, c))
        home_send(j, c).start()

    def turn(n):
        relay_edge(n)

        @pl.when(n >= LAG)
        def _():
            relay_home(n - LAG)

    def sketch_step(k, carry):
        sends = jnp.logical_and(mid == 0, k < 5)
        load_g(k).wait()
        part[k, 0] = jnp.dot(g_buf[k], mat_out[...], preferred_element_type=jnp.float32)

        @pl.when(k == 3 * mid)
        def _():
            pl.semaphore_wait(barrier, 3 + mid)

        @pl.when(sends)
        def _():
            for c in range(pieces // 2):
                edge_send(k, c).start()

        load_x(k).wait()
        part[k, 1] = jnp.dot(x_buf[k], mat_in[...], preferred_element_type=jnp.float32)

        @pl.when(sends)
        def _():
            for c in range(pieces // 2, pieces):
                edge_send(k, c).start()

        @pl.when(jnp.logical_and(mid == 1, k >= 3))
        def _():
            for n in range(2):
                turn(2 * (k - 3) + n)

        return carry

    lax.fori_loop(0, count, sketch_step, 0)
    for k in range(gram_parts):
        load_gram(k).start()

    def split(value):
        upper = value.astype(jnp.bfloat16)
        return upper, (value - upper.astype(jnp.float32)).astype(jnp.bfloat16)

    def project(k, slot):
        left, left_low = split(part[k, 0])
        right, right_low = split(part[k, 1])
        proj[slot] = lax.dot_general(
            jnp.concatenate([left, left, left_low]),
            jnp.concatenate([right, right_low, right]),
            (((0,), (0,)), ((), ())),
            preferred_element_type=jnp.float32,
        )

    def place(rep, col, i):
        return (rep * 2 + col) * count + i

    def rows_copy(slot, i, d, c):
        z = (me, 3 - 3 * side, far_mid, own_edge + own_mid - me)[d]
        col = my_col + c * (1 - 2 * my_col)
        return pltpu.make_async_remote_copy(
            src_ref=proj.at[slot, pl.ds(pl.multiple_of(z * block_p, block_p), block_p), :],
            dst_ref=allp.at[place(my_rep, my_col, i)],
            send_sem=send_rows.at[slot, d, c],
            recv_sem=recv_rows.at[my_col, i],
            device_id={"hidden": z, "cols": col},
            device_id_type=MESH,
        )

    def forward(i, n):
        block = allp.at[place(my_rep, my_col, i)]
        return pltpu.make_async_remote_copy(
            src_ref=block,
            dst_ref=block,
            send_sem=send_fwd.at[n],
            recv_sem=recv_rows.at[my_col, i],
            device_id={"cols": 1 - my_col},
            device_id_type=MESH,
        )

    def rows_arrived(col, i):
        block = allp.at[place(my_rep, col, i)]
        return pltpu.make_async_remote_copy(
            src_ref=block,
            dst_ref=block,
            send_sem=send_fwd.at[0],
            recv_sem=recv_rows.at[col, i],
            device_id={"cols": 1 - my_col},
            device_id_type=MESH,
        )

    def row_sends(late):
        both = [(d, c) for d in (1, 2, 3, 0) for c in (1, 0) if (d, c) != (0, 0)]
        return both if late else [(d, c) for d, c in both if d == 0 or c == 0]

    def keep(slot, i):
        allp[place(my_rep, my_col, i)] = proj[slot, pl.ds(pl.multiple_of(me * block_p, block_p), block_p), :]

    @pl.when(mid == 1)
    def _():
        def later(n, carry):
            turn(n)
            return carry

        lax.fori_loop(2 * (count - 3), 4 * pieces, later, 0)

        def rest(n, carry):
            relay_home(n)
            return carry

        lax.fori_loop(4 * pieces - LAG, 3 * pieces, rest, 0)
        for c in range(pieces):
            edge_arrived(4, c).wait_recv()
            far_arrived(3, c).wait_recv()
            add(4, c, cut(land_edge, 4, c))
            add(4, c, cut(land_far, 3, c))
        project(4, 0)
        for d, c in row_sends(True):
            rows_copy(0, 3 + side, d, c).start()
        keep(0, 3 + side)

    @pl.when(mid == 0)
    def _():
        def own(j, carry):
            for c in range(pieces):
                far_arrived(j, c).wait_recv()
                add(5 + j, c, cut(land_far, j, c))
            project(5 + j, j)
            i = example(5 + j)

            @pl.when(j == 0)
            def _():
                edge_send(4, pieces - 1).wait_send()

            @pl.when(j == 2)
            def _():
                for d in (1, 2, 3):
                    rows_copy(j, i, d, 1).start()

            for d in (1, 2, 3):
                rows_copy(j, i, d, 0).start()
            rows_copy(j, i, 0, 1).start()
            keep(j, i)
            return carry

        lax.fori_loop(0, 3, own, 0)

    owner = [0, 0, 0, 1, 2, 3, 3, 3]
    early = (1, 2, 5, 6)
    for n, i in enumerate(early):
        @pl.when(me != owner[i])
        def _():
            rows_arrived(my_col, i).wait_recv()
            forward(i, n).start()

    for i in range(count):
        if i not in early:
            @pl.when(me != owner[i])
            def _():
                rows_arrived(my_col, i).wait_recv()

    def core_copy(rep, col):
        block = allp.at[pl.ds((rep * 2 + col) * count, count)]
        return pltpu.make_async_remote_copy(
            src_ref=block,
            dst_ref=block,
            send_sem=send_core.at[col],
            recv_sem=recv_core.at[col],
            device_id={"rep": 1 - my_rep},
            device_id_type=MESH,
        )

    def widen(rep):
        first = pl.multiple_of(rep * 2 * count, 2 * count)
        for p in range(block_p):
            rows = allp[pl.ds(first, 2 * count), p, :]
            upper = rows.astype(jnp.bfloat16)
            wide[pl.ds(first, 2 * count), p * SKETCH : (p + 1) * SKETCH] = upper
            lower = (rows - upper.astype(jnp.float32)).astype(jnp.bfloat16)
            wide[pl.ds(4 * count + first, 2 * count), p * SKETCH : (p + 1) * SKETCH] = lower

    core_copy(my_rep, my_col).start()
    for i in range(count):
        rows_arrived(1 - my_col, i).wait_recv()
    core_copy(my_rep, 1 - my_col).start()

    def widen_step(n, carry):
        @pl.when(n == 1)
        def _():
            for col in range(2):
                core_copy(1 - my_rep, col).wait_recv()

        widen(my_rep + n * (1 - 2 * my_rep))
        return carry

    lax.fori_loop(0, 2, widen_step, 0)
    for k in range(gram_parts):
        load_gram(k).wait()

    examples = 4 * count
    per = chunks // HIDDEN

    def sum_send(n, m, z):
        return pltpu.make_async_remote_copy(
            src_ref=psum.at[n],
            dst_ref=sum_land.at[m],
            send_sem=send_sum.at[n],
            recv_sem=recv_sum.at[m],
            device_id={"hidden": z},
            device_id_type=MESH,
        )

    def sum_arrived(m):
        return pltpu.make_async_remote_copy(
            src_ref=psum.at[0],
            dst_ref=sum_land.at[m],
            send_sem=send_sum.at[0],
            recv_sem=recv_sum.at[m],
            device_id={"rep": 1 - my_rep},
            device_id_type=MESH,
        )

    def kind(d, value):
        return 1 - (lax.rem(d + HIDDEN - value, HIDDEN) + HIDDEN - 1) // HIDDEN

    far_edge, neighbour = 3 - 3 * side, own_edge + own_mid - me

    def gram_step(n, carry):
        d = n // per
        place_d = kind(d, mid * 2) * far_mid + kind(d, 1 - mid) * far_edge + kind(d, 2 - mid) * neighbour + kind(d, 3) * me
        column = pl.multiple_of((place_d * per + lax.rem(n, per)) * step_cols, step_cols)
        both = jnp.dot(wide[...], gram_buf[:, pl.ds(column, step_cols)], preferred_element_type=jnp.float32)
        total = both[:examples] + both[examples:]
        for rep in range(2):
            for col in range(2):
                a, b = (rep * 2 + col) * count, (col * 2 + rep) * count
                psum[n, b : b + count, :] = total[a : a + count]

        m = lax.rem(n, per)

        @pl.when(jnp.logical_and(mid == 0, d == 0))
        def _():
            sum_send(n, m, own_mid).start()

        @pl.when(d == 1 - mid)
        def _():
            sum_send(n, (2 - mid) * per + m, far_edge).start()

        @pl.when(d == 2 - mid)
        def _():
            sum_send(n, (1 - mid) * per + m, neighbour).start()

        @pl.when(jnp.logical_and(mid == 1, d == 2))
        def _():
            sum_arrived(m).wait_recv()
            psum[n] = psum[n] + sum_land[m]
            sum_send(n, 2 * per + m, far_mid).start()

        return carry

    lax.fori_loop(0, chunks, gram_step, 0)

    for col in range(2):
        core_copy(my_rep, col).wait_send()

    @pl.when(mid == 0)
    def _():
        for c in range(pieces):
            for k in range(5):
                if (k, c) != (4, pieces - 1):
                    edge_send(k, c).wait_send()
        for j in range(3):
            for d, c in row_sends(j == 2):
                rows_copy(j, 0, d, c).wait_send()

    @pl.when(mid == 1)
    def _():
        for c in range(pieces):
            for k in range(4):
                far_send(k, c).wait_send()
            for j in range(3):
                home_send(j, c).wait_send()
        for d, c in row_sends(True):
            rows_copy(0, 0, d, c).wait_send()

    for n in range(3 * per):
        sum_send(n, 0, neighbour).wait_send()

    for n, i in enumerate(early):
        @pl.when(me != owner[i])
        def _():
            forward(i, n).wait_send()

    for m in range(per):
        @pl.when(mid == 0)
        def _():
            sum_arrived(m).wait_recv()
            psum[3 * per + m] = psum[3 * per + m] + sum_land[m]

        sum_arrived(2 * per + m).wait_recv()
        sum_arrived(per + m).wait_recv()
        out_ref[:, m * step_cols : (m + 1) * step_cols] = psum[3 * per + m] + sum_land[2 * per + m] + sum_land[per + m]


def fused(inputs, grads, in_signs, out_signs, in_rows, out_rows, inv_gram):
    count = inputs.shape[0] // SEQ
    block_p = SKETCH // HIDDEN
    examples = 4 * count
    share = inv_gram.shape[1] // HIDDEN
    chunks = inv_gram.shape[1] // STEP
    f32 = jnp.float32
    dma = pltpu.SemaphoreType.DMA
    vmem = pl.BlockSpec(memory_space=pltpu.VMEM)
    hbm = pl.BlockSpec(memory_space=pl.ANY)
    return pl.pallas_call(
        fused_kernel,
        out_shape=pltpu.VMEM((examples, share), f32),
        in_specs=[hbm] * 7,
        out_specs=vmem,
        scratch_shapes=[
            pltpu.VMEM((inputs.shape[1] // LANES, LANES), jnp.int32),
            pltpu.VMEM((grads.shape[1] // LANES, LANES), jnp.int32),
            pltpu.VMEM((1, SKETCH), jnp.int32),
            pltpu.VMEM((1, SKETCH), jnp.int32),
            dma((4,)),
            pltpu.VMEM((count, SEQ, inputs.shape[1]), jnp.bfloat16),
            pltpu.VMEM((count, SEQ, grads.shape[1]), jnp.bfloat16),
            pltpu.VMEM(inv_gram.shape, jnp.bfloat16),
            pltpu.VMEM((inputs.shape[1], SKETCH), jnp.bfloat16),
            pltpu.VMEM((grads.shape[1], SKETCH), jnp.bfloat16),
            pltpu.VMEM((count, 2, SEQ, SKETCH), f32),
            pltpu.VMEM((5, 2, SEQ, SKETCH), f32),
            pltpu.VMEM((4, 2, SEQ, SKETCH), f32),
            pltpu.VMEM((3, SKETCH, SKETCH), f32),
            pltpu.VMEM((examples, block_p, SKETCH), f32),
            pltpu.VMEM((2 * examples, block_p * SKETCH), jnp.bfloat16),
            pltpu.VMEM((chunks, examples, STEP), f32),
            pltpu.VMEM((3 * chunks // HIDDEN, examples, STEP), f32),
            dma((count,)),
            dma((count,)),
            dma((4,)),
            dma((count, PIECES)),
            dma((5, PIECES)),
            dma((4, PIECES)),
            dma((3, HIDDEN, 2)),
            dma((4,)),
            dma((2, count)),
            dma((2,)),
            dma((2,)),
            dma((chunks,)),
            dma((3 * chunks // HIDDEN,)),
        ],
        compiler_params=pltpu.CompilerParams(
            collective_id=0, has_side_effects=True, vmem_limit_bytes=63 << 20
        ),
    )(
        inputs,
        grads,
        in_signs.reshape(inputs.shape[1] // LANES, LANES),
        out_signs.reshape(grads.shape[1] // LANES, LANES),
        in_rows.reshape(1, SKETCH),
        out_rows.reshape(1, SKETCH),
        inv_gram,
    )


def plain_sketch(values, signs, rows, width, shard):
    inner = width // HAD
    local_high = values.shape[1] // inner
    high, low = rows // inner, rows % inner
    feature = jnp.arange(values.shape[1], dtype=jnp.int32)
    sources = shard * local_high + feature // inner
    sign = (1 - 2 * had_parity(high[None, :], sources[:, None])) * signs[:, None]
    hit = (feature % inner)[:, None] == low[None, :]
    matrix = jnp.where(hit, sign.astype(jnp.float32) / math.sqrt(HAD), 0.0)
    return jnp.dot(values, matrix.astype(jnp.bfloat16), preferred_element_type=jnp.float32)


def plain(inputs, grads, in_signs, out_signs, in_rows, out_rows, inv_gram):
    shard = lax.axis_index("hidden")
    out_part = plain_sketch(grads, out_signs, out_rows, OUT_W, shard)
    in_part = plain_sketch(inputs, in_signs, in_rows, IN_W, shard)
    block_p = inv_gram.shape[0] // SKETCH
    count = inputs.shape[0] // SEQ
    out_mine = lax.psum_scatter(out_part, "hidden", scatter_dimension=1, tiled=True)
    in_sketch = lax.psum(in_part, "hidden")
    projected = jnp.einsum(
        "esp,esq->epq",
        out_mine.reshape(count, SEQ, block_p),
        in_sketch.reshape(count, SEQ, SKETCH),
        precision=lax.Precision.HIGHEST,
    )
    projected = projected.reshape(count, block_p * SKETCH)
    partial_out = jnp.dot(
        lax.all_gather(projected, ("cols", "rep"), axis=0, tiled=True),
        inv_gram.astype(jnp.float32),
        precision=lax.Precision.HIGHEST,
        preferred_element_type=jnp.float32,
    )
    return lax.psum_scatter(partial_out, "hidden", scatter_dimension=1, tiled=True)


def solution(mesh):
    dims = tuple(mesh.shape[name] for name in ("hidden", "cols", "rep"))

    def on_device(inputs, *rest):
        if dims == (HIDDEN, 2, 2) and inputs.shape[0] == 8 * SEQ:
            return fused(inputs, *rest)
        return plain(inputs, *rest)

    return jax.shard_map(
        on_device,
        mesh=mesh,
        in_specs=(
            P(("groups", "cols", "rep"), "hidden"),
            P(("groups", "cols", "rep"), "hidden"),
            P("hidden"),
            P("hidden"),
            P(),
            P(),
            P("hidden", ("cols", "rep")),
        ),
        out_specs=P("groups", ("cols", "rep", "hidden")),
        check_vma=False,
    )
```

```python
import functools
import math

import jax
import jax.numpy as jnp
from jax import lax
from jax.experimental import pallas as pl
from jax.experimental.pallas import tpu as pltpu
from jax.sharding import PartitionSpec as P

IN_W = 28672
OUT_W = 8192
HAD = 64
SKETCH = 128
SEQ = 128
LANES = 128
HIDDEN = 4
STEP = 512
PIECES = 4
LAG = 5
MESH = pl.DeviceIdType.MESH


def had_parity(left, right):
    both = jnp.bitwise_and(left, right)
    for shift in (4, 2, 1):
        both = jnp.bitwise_xor(both, jnp.right_shift(both, shift))
    return jnp.bitwise_and(both, 1)


def split_rows(rows, inner):
    high = jnp.floor((rows.astype(jnp.float32) + 0.5) * (1.0 / inner)).astype(jnp.int32)
    return high, rows - high * inner


def build_matrix(rows_ref, sign_ref, out_ref, shard, width):
    inner = width // HAD
    local_high = out_ref.shape[0] // inner
    high, low = split_rows(rows_ref[...], inner)
    hit = lax.broadcasted_iota(jnp.int32, (inner, SKETCH), 0) == low
    onehot = jnp.where(hit, 1.0, 0.0)
    sign = sign_ref[...].astype(jnp.float32).astype(jnp.bfloat16)
    line = lax.broadcasted_iota(jnp.int32, (sign.shape[0], SKETCH), 0)
    lane = lax.broadcasted_iota(jnp.int32, (LANES, SKETCH), 0)
    picked = {}
    for h in range(local_high):
        first, offset = divmod(h * inner, LANES)
        at = offset + low
        if offset not in picked:
            pick = jnp.where(lane == jnp.bitwise_and(at, LANES - 1), 1.0, 0.0).astype(jnp.bfloat16)
            picked[offset] = jnp.dot(sign, pick, preferred_element_type=jnp.float32)
        own = line == first + jnp.right_shift(at, LANES.bit_length() - 1)
        coef = jnp.sum(jnp.where(own, picked[offset], 0.0), axis=0, keepdims=True)
        parity = had_parity(high, shard * local_high + h)
        coef = coef * (1 - 2 * parity).astype(jnp.float32) * (1.0 / math.sqrt(HAD))
        out_ref[h * inner : (h + 1) * inner, :] = (onehot * coef).astype(jnp.bfloat16)


def fused_kernel(
    x_ref,
    g_ref,
    in_sign_ref,
    out_sign_ref,
    in_rows_ref,
    out_rows_ref,
    gram_ref,
    out_ref,
    in_sign,
    out_sign,
    in_rows,
    out_rows,
    small_sem,
    x_buf,
    g_buf,
    gram_buf,
    mat_in,
    mat_out,
    part,
    land_edge,
    land_far,
    proj,
    allp,
    wide,
    psum,
    sum_land,
    x_sem,
    g_sem,
    gram_sem,
    send_part,
    recv_edge,
    recv_far,
    send_rows,
    send_fwd,
    recv_rows,
    send_core,
    recv_core,
    send_sum,
    recv_sum,
):
    me = lax.axis_index("hidden")
    my_col = lax.axis_index("cols")
    my_rep = lax.axis_index("rep")
    count = x_buf.shape[0]
    side = me // 2
    mid = lax.rem((me + 1) // 2, 2)
    own_edge, own_mid, far_mid = 3 * side, 1 + side, 2 - side
    block_p = SKETCH // HIDDEN
    chunks = psum.shape[0]
    step_cols = psum.shape[2]

    def example(k):
        early = 1 - (k + count - 3) // count
        label = count - 1 - k + early * (2 * k - 2)
        return label + side * (count - 1 - 2 * label)

    def load_x(k):
        row = pl.multiple_of(example(k) * SEQ, SEQ)
        return pltpu.make_async_copy(x_ref.at[pl.ds(row, SEQ)], x_buf.at[k], x_sem.at[k])

    def load_g(k):
        row = pl.multiple_of(example(k) * SEQ, SEQ)
        return pltpu.make_async_copy(g_ref.at[pl.ds(row, SEQ)], g_buf.at[k], g_sem.at[k])

    gram_parts = gram_sem.shape[0]
    gram_rows = gram_ref.shape[0] // gram_parts

    def load_gram(k):
        where = pl.ds(k * gram_rows, gram_rows)
        return pltpu.make_async_copy(gram_ref.at[where], gram_buf.at[where], gram_sem.at[k])

    small = [(out_rows_ref, out_rows), (out_sign_ref, out_sign), (in_rows_ref, in_rows), (in_sign_ref, in_sign)]
    loads = [pltpu.make_async_copy(far, near, small_sem.at[n]) for n, (far, near) in enumerate(small)]
    for load in loads:
        load.start()
    load_g(0).start()
    load_x(0).start()

    barrier = pltpu.get_barrier_semaphore()
    pl.semaphore_signal(barrier, inc=1, device_id={"rep": 1 - my_rep}, device_id_type=MESH)
    pl.semaphore_signal(barrier, inc=1, device_id={"cols": 1 - my_col}, device_id_type=MESH)
    pl.semaphore_signal(barrier, inc=1, device_id={"hidden": own_edge + own_mid - me}, device_id_type=MESH)

    @pl.when(mid == 1)
    def _():
        pl.semaphore_signal(barrier, inc=1, device_id={"hidden": far_mid}, device_id_type=MESH)

    for load in loads:
        load.wait()
    for k in range(1, count):
        load_g(k).start()
        load_x(k).start()
    build_matrix(out_rows, out_sign, mat_out, me, OUT_W)
    build_matrix(in_rows, in_sign, mat_in, me, IN_W)

    pieces = send_part.shape[1]
    piece = 2 * SEQ // pieces

    def cut(ref, k, c):
        row = pl.multiple_of(lax.rem(c, pieces // 2) * piece, piece)
        return ref.at[k, c // (pieces // 2), pl.ds(row, piece)]

    def edge_send(k, c):
        return pltpu.make_async_remote_copy(
            src_ref=cut(part, k, c),
            dst_ref=cut(land_edge, k, c),
            send_sem=send_part.at[k, c],
            recv_sem=recv_edge.at[k, c],
            device_id={"hidden": own_mid},
            device_id_type=MESH,
        )

    def far_send(k, c):
        return pltpu.make_async_remote_copy(
            src_ref=cut(part, k, c),
            dst_ref=cut(land_far, k, c),
            send_sem=send_part.at[k, c],
            recv_sem=recv_far.at[k, c],
            device_id={"hidden": far_mid},
            device_id_type=MESH,
        )

    def home_send(j, c):
        return pltpu.make_async_remote_copy(
            src_ref=cut(part, 5 + j, c),
            dst_ref=cut(land_far, j, c),
            send_sem=send_part.at[5 + j, c],
            recv_sem=recv_far.at[j, c],
            device_id={"hidden": own_edge},
            device_id_type=MESH,
        )

    def edge_arrived(k, c):
        return pltpu.make_async_remote_copy(
            src_ref=cut(part, k, c),
            dst_ref=cut(land_edge, k, c),
            send_sem=send_part.at[k, c],
            recv_sem=recv_edge.at[k, c],
            device_id={"rep": 1 - my_rep},
            device_id_type=MESH,
        )

    def far_arrived(k, c):
        return pltpu.make_async_remote_copy(
            src_ref=cut(part, k, c),
            dst_ref=cut(land_far, k, c),
            send_sem=send_part.at[k, c],
            recv_sem=recv_far.at[k, c],
            device_id={"rep": 1 - my_rep},
            device_id_type=MESH,
        )

    def add(k, c, landed):
        here = cut(part, k, c)
        here[...] = here[...] + landed[...]

    def relay_edge(n):
        k, c = n // pieces, lax.rem(n, pieces)
        edge_arrived(k, c).wait_recv()
        add(k, c, cut(land_edge, k, c))
        far_send(k, c).start()

    def relay_home(n):
        j, c = n // pieces, lax.rem(n, pieces)
        far_arrived(j, c).wait_recv()
        add(5 + j, c, cut(land_far, j, c))
        home_send(j, c).start()

    def turn(n):
        relay_edge(n)

        @pl.when(n >= LAG)
        def _():
            relay_home(n - LAG)

    def sketch_step(k, carry):
        sends = jnp.logical_and(mid == 0, k < 5)
        load_g(k).wait()
        part[k, 0] = jnp.dot(g_buf[k], mat_out[...], preferred_element_type=jnp.float32)

        @pl.when(k == 3 * mid)
        def _():
            pl.semaphore_wait(barrier, 3 + mid)

        @pl.when(sends)
        def _():
            for c in range(pieces // 2):
                edge_send(k, c).start()

        load_x(k).wait()
        part[k, 1] = jnp.dot(x_buf[k], mat_in[...], preferred_element_type=jnp.float32)

        @pl.when(sends)
        def _():
            for c in range(pieces // 2, pieces):
                edge_send(k, c).start()

        @pl.when(jnp.logical_and(mid == 1, k >= 3))
        def _():
            for n in range(2):
                turn(2 * (k - 3) + n)

        return carry

    lax.fori_loop(0, count, sketch_step, 0)
    for k in range(gram_parts):
        load_gram(k).start()

    def split(value):
        upper = value.astype(jnp.bfloat16)
        return upper, (value - upper.astype(jnp.float32)).astype(jnp.bfloat16)

    def project(k, slot):
        left, left_low = split(part[k, 0])
        right, right_low = split(part[k, 1])
        proj[slot] = lax.dot_general(
            jnp.concatenate([left, left, left_low]),
            jnp.concatenate([right, right_low, right]),
            (((0,), (0,)), ((), ())),
            preferred_element_type=jnp.float32,
        )

    def place(rep, col, i):
        return (rep * 2 + col) * count + i

    def rows_copy(slot, i, d, c):
        z = (me, 3 - 3 * side, far_mid, own_edge + own_mid - me)[d]
        col = my_col + c * (1 - 2 * my_col)
        return pltpu.make_async_remote_copy(
            src_ref=proj.at[slot, pl.ds(pl.multiple_of(z * block_p, block_p), block_p), :],
            dst_ref=allp.at[place(my_rep, my_col, i)],
            send_sem=send_rows.at[slot, d, c],
            recv_sem=recv_rows.at[my_col, i],
            device_id={"hidden": z, "cols": col},
            device_id_type=MESH,
        )

    def forward(i, n):
        block = allp.at[place(my_rep, my_col, i)]
        return pltpu.make_async_remote_copy(
            src_ref=block,
            dst_ref=block,
            send_sem=send_fwd.at[n],
            recv_sem=recv_rows.at[my_col, i],
            device_id={"cols": 1 - my_col},
            device_id_type=MESH,
        )

    def rows_arrived(col, i):
        block = allp.at[place(my_rep, col, i)]
        return pltpu.make_async_remote_copy(
            src_ref=block,
            dst_ref=block,
            send_sem=send_fwd.at[0],
            recv_sem=recv_rows.at[col, i],
            device_id={"cols": 1 - my_col},
            device_id_type=MESH,
        )

    def row_sends(late):
        both = [(d, c) for d in (1, 2, 3, 0) for c in (1, 0) if (d, c) != (0, 0)]
        return both if late else [(d, c) for d, c in both if d == 0 or c == 0]

    def keep(slot, i):
        allp[place(my_rep, my_col, i)] = proj[slot, pl.ds(pl.multiple_of(me * block_p, block_p), block_p), :]

    @pl.when(mid == 1)
    def _():
        def later(n, carry):
            turn(n)
            return carry

        lax.fori_loop(2 * (count - 3), 4 * pieces, later, 0)

        def rest(n, carry):
            relay_home(n)
            return carry

        lax.fori_loop(4 * pieces - LAG, 3 * pieces, rest, 0)
        for c in range(pieces):
            edge_arrived(4, c).wait_recv()
            far_arrived(3, c).wait_recv()
            add(4, c, cut(land_edge, 4, c))
            add(4, c, cut(land_far, 3, c))
        project(4, 0)
        for d, c in row_sends(True):
            rows_copy(0, 3 + side, d, c).start()
        keep(0, 3 + side)

    @pl.when(mid == 0)
    def _():
        def own(j, carry):
            for c in range(pieces):
                far_arrived(j, c).wait_recv()
                add(5 + j, c, cut(land_far, j, c))
            project(5 + j, j)
            i = example(5 + j)

            @pl.when(j == 0)
            def _():
                edge_send(4, pieces - 1).wait_send()

            @pl.when(j == 2)
            def _():
                for d in (1, 2, 3):
                    rows_copy(j, i, d, 1).start()

            for d in (1, 2, 3):
                rows_copy(j, i, d, 0).start()
            rows_copy(j, i, 0, 1).start()
            keep(j, i)
            return carry

        lax.fori_loop(0, 3, own, 0)

    owner = [0, 0, 0, 1, 2, 3, 3, 3]
    early = (1, 2, 5, 6)
    for n, i in enumerate(early):
        @pl.when(me != owner[i])
        def _():
            rows_arrived(my_col, i).wait_recv()
            forward(i, n).start()

    for i in range(count):
        if i not in early:
            @pl.when(me != owner[i])
            def _():
                rows_arrived(my_col, i).wait_recv()

    def core_copy(rep, col):
        block = allp.at[pl.ds((rep * 2 + col) * count, count)]
        return pltpu.make_async_remote_copy(
            src_ref=block,
            dst_ref=block,
            send_sem=send_core.at[col],
            recv_sem=recv_core.at[col],
            device_id={"rep": 1 - my_rep},
            device_id_type=MESH,
        )

    def widen(rep):
        first = pl.multiple_of(rep * 2 * count, 2 * count)
        for p in range(block_p):
            rows = allp[pl.ds(first, 2 * count), p, :]
            upper = rows.astype(jnp.bfloat16)
            wide[pl.ds(first, 2 * count), p * SKETCH : (p + 1) * SKETCH] = upper
            lower = (rows - upper.astype(jnp.float32)).astype(jnp.bfloat16)
            wide[pl.ds(4 * count + first, 2 * count), p * SKETCH : (p + 1) * SKETCH] = lower

    core_copy(my_rep, my_col).start()
    for i in range(count):
        rows_arrived(1 - my_col, i).wait_recv()
    core_copy(my_rep, 1 - my_col).start()

    def widen_step(n, carry):
        @pl.when(n == 1)
        def _():
            for col in range(2):
                core_copy(1 - my_rep, col).wait_recv()

        widen(my_rep + n * (1 - 2 * my_rep))
        return carry

    lax.fori_loop(0, 2, widen_step, 0)
    for k in range(gram_parts):
        load_gram(k).wait()

    examples = 4 * count
    per = chunks // HIDDEN

    def sum_send(n, m, z):
        return pltpu.make_async_remote_copy(
            src_ref=psum.at[n],
            dst_ref=sum_land.at[m],
            send_sem=send_sum.at[n],
            recv_sem=recv_sum.at[m],
            device_id={"hidden": z},
            device_id_type=MESH,
        )

    def sum_arrived(m):
        return pltpu.make_async_remote_copy(
            src_ref=psum.at[0],
            dst_ref=sum_land.at[m],
            send_sem=send_sum.at[0],
            recv_sem=recv_sum.at[m],
            device_id={"rep": 1 - my_rep},
            device_id_type=MESH,
        )

    def kind(d, value):
        return 1 - (lax.rem(d + HIDDEN - value, HIDDEN) + HIDDEN - 1) // HIDDEN

    far_edge, neighbour = 3 - 3 * side, own_edge + own_mid - me

    def gram_step(n, carry):
        d = n // per
        place_d = kind(d, mid * 2) * far_mid + kind(d, 1 - mid) * far_edge + kind(d, 2 - mid) * neighbour + kind(d, 3) * me
        column = pl.multiple_of((place_d * per + lax.rem(n, per)) * step_cols, step_cols)
        both = jnp.dot(wide[...], gram_buf[:, pl.ds(column, step_cols)], preferred_element_type=jnp.float32)
        total = both[:examples] + both[examples:]
        for rep in range(2):
            for col in range(2):
                a, b = (rep * 2 + col) * count, (col * 2 + rep) * count
                psum[n, b : b + count, :] = total[a : a + count]

        m = lax.rem(n, per)

        @pl.when(jnp.logical_and(mid == 0, d == 0))
        def _():
            sum_send(n, m, own_mid).start()

        @pl.when(d == 1 - mid)
        def _():
            sum_send(n, (2 - mid) * per + m, far_edge).start()

        @pl.when(d == 2 - mid)
        def _():
            sum_send(n, (1 - mid) * per + m, neighbour).start()

        @pl.when(jnp.logical_and(mid == 1, d == 2))
        def _():
            sum_arrived(m).wait_recv()
            psum[n] = psum[n] + sum_land[m]
            sum_send(n, 2 * per + m, far_mid).start()

        return carry

    lax.fori_loop(0, chunks, gram_step, 0)

    for col in range(2):
        core_copy(my_rep, col).wait_send()

    @pl.when(mid == 0)
    def _():
        for c in range(pieces):
            for k in range(5):
                if (k, c) != (4, pieces - 1):
                    edge_send(k, c).wait_send()
        for j in range(3):
            for d, c in row_sends(j == 2):
                rows_copy(j, 0, d, c).wait_send()

    @pl.when(mid == 1)
    def _():
        for c in range(pieces):
            for k in range(4):
                far_send(k, c).wait_send()
            for j in range(3):
                home_send(j, c).wait_send()
        for d, c in row_sends(True):
            rows_copy(0, 0, d, c).wait_send()

    for n in range(3 * per):
        sum_send(n, 0, neighbour).wait_send()

    for n, i in enumerate(early):
        @pl.when(me != owner[i])
        def _():
            forward(i, n).wait_send()

    for m in range(per):
        @pl.when(mid == 0)
        def _():
            sum_arrived(m).wait_recv()
            psum[3 * per + m] = psum[3 * per + m] + sum_land[m]

        sum_arrived(2 * per + m).wait_recv()
        sum_arrived(per + m).wait_recv()
        out_ref[:, m * step_cols : (m + 1) * step_cols] = psum[3 * per + m] + sum_land[2 * per + m] + sum_land[per + m]


def fused(inputs, grads, in_signs, out_signs, in_rows, out_rows, inv_gram):
    count = inputs.shape[0] // SEQ
    block_p = SKETCH // HIDDEN
    examples = 4 * count
    share = inv_gram.shape[1] // HIDDEN
    chunks = inv_gram.shape[1] // STEP
    f32 = jnp.float32
    dma = pltpu.SemaphoreType.DMA
    vmem = pl.BlockSpec(memory_space=pltpu.VMEM)
    hbm = pl.BlockSpec(memory_space=pl.ANY)
    return pl.pallas_call(
        fused_kernel,
        out_shape=pltpu.VMEM((examples, share), f32),
        in_specs=[hbm] * 7,
        out_specs=vmem,
        scratch_shapes=[
            pltpu.VMEM((inputs.shape[1] // LANES, LANES), jnp.int32),
            pltpu.VMEM((grads.shape[1] // LANES, LANES), jnp.int32),
            pltpu.VMEM((1, SKETCH), jnp.int32),
            pltpu.VMEM((1, SKETCH), jnp.int32),
            dma((4,)),
            pltpu.VMEM((count, SEQ, inputs.shape[1]), jnp.bfloat16),
            pltpu.VMEM((count, SEQ, grads.shape[1]), jnp.bfloat16),
            pltpu.VMEM(inv_gram.shape, jnp.bfloat16),
            pltpu.VMEM((inputs.shape[1], SKETCH), jnp.bfloat16),
            pltpu.VMEM((grads.shape[1], SKETCH), jnp.bfloat16),
            pltpu.VMEM((count, 2, SEQ, SKETCH), f32),
            pltpu.VMEM((5, 2, SEQ, SKETCH), f32),
            pltpu.VMEM((4, 2, SEQ, SKETCH), f32),
            pltpu.VMEM((3, SKETCH, SKETCH), f32),
            pltpu.VMEM((examples, block_p, SKETCH), f32),
            pltpu.VMEM((2 * examples, block_p * SKETCH), jnp.bfloat16),
            pltpu.VMEM((chunks, examples, STEP), f32),
            pltpu.VMEM((3 * chunks // HIDDEN, examples, STEP), f32),
            dma((count,)),
            dma((count,)),
            dma((4,)),
            dma((count, PIECES)),
            dma((5, PIECES)),
            dma((4, PIECES)),
            dma((3, HIDDEN, 2)),
            dma((4,)),
            dma((2, count)),
            dma((2,)),
            dma((2,)),
            dma((chunks,)),
            dma((3 * chunks // HIDDEN,)),
        ],
        compiler_params=pltpu.CompilerParams(
            collective_id=0, has_side_effects=True, vmem_limit_bytes=63 << 20
        ),
    )(
        inputs,
        grads,
        in_signs.reshape(inputs.shape[1] // LANES, LANES),
        out_signs.reshape(grads.shape[1] // LANES, LANES),
        in_rows.reshape(1, SKETCH),
        out_rows.reshape(1, SKETCH),
        inv_gram,
    )


def plain_sketch(values, signs, rows, width, shard):
    inner = width // HAD
    local_high = values.shape[1] // inner
    high, low = rows // inner, rows % inner
    feature = jnp.arange(values.shape[1], dtype=jnp.int32)
    sources = shard * local_high + feature // inner
    sign = (1 - 2 * had_parity(high[None, :], sources[:, None])) * signs[:, None]
    hit = (feature % inner)[:, None] == low[None, :]
    matrix = jnp.where(hit, sign.astype(jnp.float32) / math.sqrt(HAD), 0.0)
    return jnp.dot(values, matrix.astype(jnp.bfloat16), preferred_element_type=jnp.float32)


def plain(inputs, grads, in_signs, out_signs, in_rows, out_rows, inv_gram):
    shard = lax.axis_index("hidden")
    out_part = plain_sketch(grads, out_signs, out_rows, OUT_W, shard)
    in_part = plain_sketch(inputs, in_signs, in_rows, IN_W, shard)
    block_p = inv_gram.shape[0] // SKETCH
    count = inputs.shape[0] // SEQ
    out_mine = lax.psum_scatter(out_part, "hidden", scatter_dimension=1, tiled=True)
    in_sketch = lax.psum(in_part, "hidden")
    projected = jnp.einsum(
        "esp,esq->epq",
        out_mine.reshape(count, SEQ, block_p),
        in_sketch.reshape(count, SEQ, SKETCH),
        precision=lax.Precision.HIGHEST,
    )
    projected = projected.reshape(count, block_p * SKETCH)
    partial_out = jnp.dot(
        lax.all_gather(projected, ("cols", "rep"), axis=0, tiled=True),
        inv_gram.astype(jnp.float32),
        precision=lax.Precision.HIGHEST,
        preferred_element_type=jnp.float32,
    )
    return lax.psum_scatter(partial_out, "hidden", scatter_dimension=1, tiled=True)


def solution(mesh):
    dims = tuple(mesh.shape[name] for name in ("hidden", "cols", "rep"))

    def on_device(inputs, *rest):
        if dims == (HIDDEN, 2, 2) and inputs.shape[0] == 8 * SEQ:
            return fused(inputs, *rest)
        return plain(inputs, *rest)

    return jax.shard_map(
        on_device,
        mesh=mesh,
        in_specs=(
            P(("groups", "cols", "rep"), "hidden"),
            P(("groups", "cols", "rep"), "hidden"),
            P("hidden"),
            P("hidden"),
            P(),
            P(),
            P("hidden", ("cols", "rep")),
        ),
        out_specs=P("groups", ("cols", "rep", "hidden")),
        check_vma=False,
    )
```
